256 devices in a mesh: grp: 128 (over x, y, z), cores: 2 (over core).
Axes of the slice: x: 4, y: 4, z: 8, core: 2. Of those that a mesh axis runs over, the one named last changes fastest.
Arguments:
- invariant_fluid_quantities: float32 [8, 16384, 512], P(None, ('grp', 'cores')), may hold values from -6 to 6
- flux_derivative_matrices: float32 [3, 8, 8], replicated, may hold values from -2 to 2
- levels: int32 [16384], P(('grp', 'cores')), may hold values from 0 to 3
- neighbours: int32 [16384, 6], P(('grp', 'cores')), may hold values from -1 to 16383, as said below
- block_latitude_band: int32 [16384, 1], P(('grp', 'cores')), may hold values from 0 to 127; in each aligned block of 64 rows (0 to 63, 64 to 127, ...) at most 2 rows name the same one
- block_longitude_segment: int32 [16384], P(('grp', 'cores')), may hold values from 0 to 15
- parallel_flow_coefficients: float32 [8], replicated, may hold values from -2 to 2
Outputs:
- state_out: float32 [8, 16384, 512], P(None, ('grp', 'cores'))
- fac_grid: float32 [512, 1024], P(('grp', 'cores'))
- potential: float32 [512, 1024], P(('grp', 'cores'))
- shell_potential: float32 [16384, 128], P(('grp', 'cores'))
The draws below stay inside these ranges and needn't reach their ends.
Inputs may be any that keep to these rules, and one draw needn't show every extreme that they name: `neighbours`: each entry is -1 or a block held by the same device as the block or by the device just before or after it; device i holds blocks i * 64 to (i + 1) * 64 - 1. `block_latitude_band`: among the 64 blocks of one device no band is named more than 2 times, a bound that some block reaches.
All inputs are finite; a program needn't handle non-finite values.
Results may differ from the reference program's by a relative error of at most 0.0004.
Values sent between devices are 32-bit elements; how exact they have to be, the bound alone decides.
No kernel may reach another device: no remote copies, remote signals or barrier semaphores. Data moves between devices by JAX's collectives and lax.ppermute only.
A program may use at most 128 MiB of HBM per device.

```python
import math
import jax
import jax.numpy as jnp
import numpy as np
from jax import lax

FLUID_QUANTITIES = 8
CUBES_PER_CHIP = 64
LEVELS = 4
STEPS = 2
LAT_DEV = 2
NLON = 1024
DEGREES = 512
CUBE_COUNT = 16384
CAP = 2
NLAT = 512
SEGS = 16
N_GRP = 128
N_CORES = 2


def draw_neighbours(key, part):
    total = CUBES_PER_CHIP * N_GRP * N_CORES
    block_ids = jnp.arange(total, dtype=jnp.int32)
    owner = block_ids // CUBES_PER_CHIP
    offsets = jax.random.randint(key, (total, 6), -CUBES_PER_CHIP, 2 * CUBES_PER_CHIP, dtype=jnp.int32)
    candidate = owner[:, None] * CUBES_PER_CHIP + offsets
    result = jnp.where((candidate >= 0) & (candidate < total), candidate, -1)
    result = result.at[0, 0].set(-1)
    result = result.at[total - 2, 1].set(total - 1)
    return result.astype(jnp.int32)


def with_ends(array, own_key, low, top_value):
    shape = array.shape
    index_at = [jax.random.randint(jax.random.fold_in(own_key, axis), (), 0, shape[axis]) for axis in range(len(shape))]
    array = array.at[tuple(index_at)].set(low)
    longest = shape.index(max(shape))
    index_at[longest] = (index_at[longest] + 1) % shape[longest]
    return array.at[tuple(index_at)].set(top_value)


def block_scale(stream_key, dims, shards, smallest, high):
    def one(axis_at, shards_of):
        heights = jax.random.uniform(jax.random.fold_in(jax.random.fold_in(stream_key, 6), axis_at), (shards_of,), jnp.float32, smallest / len(shards), high / len(shards))
        return jnp.repeat(jnp.exp(heights), dims[axis_at] // shards_of).reshape((-1,) + (1,) * (len(dims) - axis_at - 1))

    level = one(*shards[0])
    for cut in shards[1:]:
        level = level * one(*cut)
    return level


def assign_block(rng, own, number, rows, count, top, bound, lean):
    sequence = jax.random.permutation(rng, count)
    crowded, common = shares(count, rows * top, bound, lean, True), shares(count, rows * top, bound, lean, False)
    places = jnp.arange(count)

    def named(tallies, turn):
        used = int((tallies > 0).sum())
        fixed = max(1, used // 4)
        moved = fixed + (places - fixed + turn * (used - fixed)) % max(1, count - fixed)
        return jnp.zeros((count,), jnp.int32).at[sequence[jnp.where(places < fixed, places, moved)]].set(jnp.asarray(tallies, jnp.int32))

    tallies = jnp.where(number % 4 == 0, named(crowded, number // 4), named(common, number - number // 4 - 1))
    mixed = jax.random.permutation(jax.random.fold_in(own, 3), count)
    giver, receiver = mixed[0:count // 2 * 2:2], mixed[1:count // 2 * 2:2]
    slack = jnp.minimum(tallies[giver] - 1, bound - tallies[receiver]) // 2
    slack = jnp.where((giver == sequence[0]) | (receiver == sequence[0]) | (tallies[receiver] == 0), 0, jnp.maximum(slack, 0))
    moved = jax.random.randint(jax.random.fold_in(own, 4), (count // 2,), 0, 1 << 20) % (slack + 1)
    tallies = tallies.at[giver].add(-moved).at[receiver].add(moved)
    items = jnp.searchsorted(jnp.cumsum(tallies), jnp.arange(rows * top), side="right").astype(jnp.int32)
    listing = items.reshape(top, rows).T
    listing = listing[jax.random.permutation(jax.random.fold_in(own, 1), rows)]
    turn = jax.random.randint(jax.random.fold_in(own, 2), (rows, 1), 0, top)
    return jnp.take_along_axis(listing, (jnp.arange(top)[None, :] + turn) % top, axis=1)


def shares(count, total, most, slope, full):
    portions = [(1 << 20) // math.isqrt(grade ** slope) + 1 for grade in range(1, count + 1)]
    largest = most if full else min(most, max(-(-total // count), total * portions[0] // sum(portions)))
    least = 1 if total - largest >= count - 1 else 0
    holding, surplus = [largest] + [least] * (count - 1), total - largest - least * (count - 1)
    while surplus > 0:
        candidates = [i for i in range(1, count) if holding[i] < largest] or [i for i in range(1, count) if holding[i] < most]
        whole, left = sum([portions[i] for i in candidates]), surplus
        for i in candidates:
            addition = min(most - holding[i], max(1, left * portions[i] // whole), surplus)
            holding[i] = holding[i] + addition
            surplus = surplus - addition
    return np.array(holding)


def normal_values(own_key, extent, spread, most, pieces=(), held_as=jnp.bfloat16):
    level = block_scale(own_key, extent, pieces, -0.22, 0.18) if pieces else 1.0
    array = jax.random.normal(own_key, extent, jnp.float32) * spread * level
    return jnp.minimum(jnp.maximum(array, -most), most).astype(held_as)


def setup_inputs(seed: int = 0) -> dict:
    key_list = jax.random.split(jax.random.key(seed), 8)
    invariant_fluid_quantities = normal_values(key_list[0], (FLUID_QUANTITIES, CUBE_COUNT, 512), 1.0, 6.0, ((1, 256),), jnp.float32)
    flux_derivative_matrices = normal_values(key_list[1], (3, FLUID_QUANTITIES, FLUID_QUANTITIES), FLUID_QUANTITIES ** -0.5, 2.0, (), jnp.float32)
    levels = with_ends(jax.random.randint(key_list[2], (CUBE_COUNT,), 0, LEVELS), jax.random.fold_in(key_list[2], 1), 0, LEVELS - 1).astype(jnp.int32)
    neighbours = draw_neighbours(jax.random.fold_in(key_list[7], 71), 0)
    block_latitude_band_keys = jax.random.split(jax.random.fold_in(key_list[4], 1), CUBE_COUNT // CUBES_PER_CHIP)
    block_latitude_band_turns = jax.random.permutation(jax.random.fold_in(key_list[4], 3), CUBE_COUNT // CUBES_PER_CHIP)
    block_latitude_band = jax.vmap(lambda own, number: assign_block(jax.random.fold_in(key_list[4], 2), own, number, CUBES_PER_CHIP, N_GRP, 1, CAP, 2))(block_latitude_band_keys, block_latitude_band_turns).reshape((CUBE_COUNT, 1))
    block_longitude_segment = with_ends(jax.random.randint(key_list[5], (CUBE_COUNT,), 0, SEGS), jax.random.fold_in(key_list[5], 1), 0, SEGS - 1).astype(jnp.int32)
    parallel_flow_coefficients = normal_values(key_list[6], (FLUID_QUANTITIES,), FLUID_QUANTITIES ** -0.5, 2.0, (), jnp.float32)
    return {"invariant_fluid_quantities": invariant_fluid_quantities, "flux_derivative_matrices": flux_derivative_matrices, "levels": levels, "neighbours": neighbours, "block_latitude_band": block_latitude_band, "block_longitude_segment": block_longitude_segment, "parallel_flow_coefficients": parallel_flow_coefficients}


COURANT = 0.3
KAPPA2 = 400.0
POT_GAIN = 2000.0
HIGHEST_PRECISION = lax.Precision.HIGHEST

def block_faces(state_in):
    state_variables, blocks = (state_in.shape[0], state_in.shape[1])
    block_cube = state_in.reshape(state_variables, blocks, 8, 8, 8)
    layers = [block_cube[:, :, 0], block_cube[:, :, 7], block_cube[:, :, :, 0], block_cube[:, :, :, 7], block_cube[:, :, :, :, 0], block_cube[:, :, :, :, 7]]
    return jnp.stack([one_layer.reshape(state_variables, blocks, 64) for one_layer in layers], axis=2)

def spread_face(values, direction):
    state_variables, blocks = (values.shape[0], values.shape[1])
    if direction == 0:
        expanded = jnp.broadcast_to(values.reshape(state_variables, blocks, 1, 64), (state_variables, blocks, 8, 64))
    elif direction == 1:
        expanded = jnp.broadcast_to(values.reshape(state_variables, blocks, 8, 1, 8), (state_variables, blocks, 8, 8, 8))
    else:
        expanded = jnp.broadcast_to(values.reshape(state_variables, blocks, 64, 1), (state_variables, blocks, 64, 8))
    return expanded.reshape(state_variables, blocks, 512)

def ghost_values(own_faces, face_table, index):
    result = []
    for face_index in range(6):
        column = index[:, face_index]
        fetched = jnp.take(face_table[:, :, face_index ^ 1], jnp.maximum(column, 0), axis=1)
        selected = jnp.where(column[None, :, None] >= 0, fetched, own_faces[:, :, face_index])
        result.append(spread_face(selected, face_index // 2))
    return result

def wave_speeds(flux_derivative_matrices):
    return lax.optimization_barrier(jnp.max(lax.optimization_barrier(jnp.sum(jnp.abs(flux_derivative_matrices), axis=2)), axis=1))

def advance(state_in, flux_derivative_matrices, speeds, rate_block, ghosts):
    position = jnp.arange(512, dtype=jnp.int32)
    change = jnp.zeros(state_in.shape, jnp.float32)
    for direction in range(3):
        stride = 64 // 8 ** direction
        coordinate = position // stride % 8
        lower_side = jnp.where(coordinate == 0, ghosts[2 * direction], jnp.roll(state_in, stride, axis=2))
        upper_side = jnp.where(coordinate == 7, ghosts[2 * direction + 1], jnp.roll(state_in, -stride, axis=2))
        difference = jnp.einsum('ij,jbp->ibp', flux_derivative_matrices[direction], upper_side - lower_side, precision=HIGHEST_PRECISION)
        change = change + 0.5 * difference - 0.5 * speeds[direction] * (upper_side - 2.0 * state_in + lower_side)
    return state_in - rate_block[None, :, None] * change

def shell_currents(state_in, parallel_flow_coefficients):
    state_variables, blocks = (state_in.shape[0], state_in.shape[1])
    inner_cells = state_in.reshape(state_variables, blocks, 64, 8)[:, :, :, 0:2]
    inner_cells = jnp.swapaxes(inner_cells, 2, 3).reshape(state_variables, blocks, 128)
    return jnp.einsum('v,vbk->bk', parallel_flow_coefficients, inner_cells, precision=HIGHEST_PRECISION)

def fourier_tables(orders):
    longitudes = jnp.arange(NLON, dtype=jnp.int32)
    phase_index = longitudes[:, None] * orders[None, :] % NLON
    angle_rad = phase_index.astype(jnp.float32) * (2.0 * math.pi / NLON)
    return (jnp.cos(angle_rad), jnp.sin(angle_rad))

def legendre_start(sine_lat, orders):
    series_k = jnp.arange(1, DEGREES, dtype=jnp.int32).astype(jnp.float32)
    log_sums = jnp.concatenate([jnp.zeros((1,), jnp.float32), jnp.cumsum(0.5 * jnp.log((2.0 * series_k + 1.0) / (2.0 * series_k)))])
    log_base = jnp.take(log_sums, orders)
    order_real = orders.astype(jnp.float32)
    return jnp.exp(0.5 * math.log(0.5) + log_base[None, :] + order_real[None, :] * jnp.log(sine_lat)[:, None])

def legendre_next(degree, orders, cosine_lat, diagonal, previous, before):
    degree_real = degree.astype(jnp.float32)
    order_real = orders.astype(jnp.float32)[None, :]
    order_int = orders[None, :]
    cosine_col = cosine_lat[:, None]
    ratio_up = jnp.sqrt(jnp.maximum(4.0 * degree_real * degree_real - 1.0, 1.0) / jnp.maximum(degree_real * degree_real - order_real * order_real, 1.0))
    lower_deg = degree_real - 1.0
    ratio_back = jnp.sqrt(jnp.maximum(lower_deg * lower_deg - order_real * order_real, 0.0) / jnp.maximum(4.0 * lower_deg * lower_deg - 1.0, 1.0))
    coef_prev = jnp.where(degree == order_int + 1, jnp.sqrt(2.0 * order_real + 3.0) * cosine_col, jnp.where(degree >= order_int + 2, ratio_up * cosine_col, 0.0))
    coef_before = jnp.where(degree >= order_int + 2, -ratio_up * ratio_back, 0.0)
    injected = jnp.where(degree == order_int, diagonal, 0.0)
    return coef_prev * previous + coef_before * before + injected

def solve_spectral(coef_re, coef_im, cosine_lat, sine_lat, weights_lat, orders):
    diagonal = legendre_start(sine_lat, orders)
    zero_state = jnp.zeros(diagonal.shape, jnp.float32)

    def one_degree(carried, degree):
        previous, before, acc_re, acc_im = carried
        present = legendre_next(degree, orders, cosine_lat, diagonal, previous, before)
        weighted = weights_lat[:, None] * present
        spec_re = lax.optimization_barrier(jnp.sum(coef_re * weighted, axis=0))
        spec_im = lax.optimization_barrier(jnp.sum(coef_im * weighted, axis=0))
        degree_real = degree.astype(jnp.float32)
        gain_deg = POT_GAIN / (degree_real * (degree_real + 1.0) + KAPPA2)
        acc_re = acc_re + (gain_deg * spec_re)[None, :] * present
        acc_im = acc_im + (gain_deg * spec_im)[None, :] * present
        return ((present, previous, acc_re, acc_im), None)
    carried, _ = lax.scan(one_degree, (zero_state, zero_state, zero_state, zero_state), jnp.arange(DEGREES, dtype=jnp.int32))
    return (carried[2], carried[3])

def reference(invariant_fluid_quantities, flux_derivative_matrices, levels, neighbours, block_latitude_band, block_longitude_segment, parallel_flow_coefficients):
    speeds = wave_speeds(flux_derivative_matrices)
    rate_block = COURANT * jnp.exp2(levels.astype(jnp.float32) - (LEVELS - 1)) / jnp.max(speeds)
    batches_list = CUBE_COUNT // CUBES_PER_CHIP
    parallel_flow_charge = invariant_fluid_quantities
    for section_index in range(STEPS):
        face_table = block_faces(parallel_flow_charge)

        def step_group(inputs):
            group_state, group_index, group_rate = inputs
            own_faces = block_faces(group_state)
            ghosts = ghost_values(own_faces, face_table, group_index)
            return advance(group_state, flux_derivative_matrices, speeds, group_rate, ghosts)
        batched_together = jnp.moveaxis(parallel_flow_charge.reshape(FLUID_QUANTITIES, batches_list, CUBES_PER_CHIP, 512), 1, 0)
        advanced_forward = lax.map(step_group, (batched_together, neighbours.reshape(batches_list, CUBES_PER_CHIP, 6), rate_block.reshape(batches_list, CUBES_PER_CHIP)))
        parallel_flow_charge = jnp.moveaxis(advanced_forward, 0, 1).reshape(FLUID_QUANTITIES, CUBE_COUNT, 512)
    patches = shell_currents(parallel_flow_charge, parallel_flow_coefficients)
    block_ids = jnp.arange(CUBE_COUNT, dtype=jnp.int32)
    core_of = block_ids // CUBES_PER_CHIP % N_CORES
    first_lat = LAT_DEV * (N_CORES * block_latitude_band[:, 0] + core_of)
    cell_k = jnp.arange(128, dtype=jnp.int32)
    lat_rows = first_lat[:, None] + cell_k[None, :] // 64
    lon_cols = block_longitude_segment[:, None] * 64 + cell_k[None, :] % 64
    flat_cells = (lat_rows * NLON + lon_cols).astype(jnp.int32)
    fac_grid = jax.ops.segment_sum(patches.reshape(-1), flat_cells.reshape(-1), num_segments=NLAT * NLON).reshape(NLAT, NLON)
    orders = jnp.arange(DEGREES, dtype=jnp.int32)
    cos_table, sin_table = fourier_tables(orders)
    coef_re = jnp.dot(fac_grid, cos_table, precision=HIGHEST_PRECISION) / NLON
    coef_im = -jnp.dot(fac_grid, sin_table, precision=HIGHEST_PRECISION) / NLON
    lat_ids = jnp.arange(NLAT, dtype=jnp.int32)
    colatitude = (lat_ids.astype(jnp.float32) + 0.5) * (math.pi / NLAT)
    cosine_lat = jnp.cos(colatitude)
    sine_lat = jnp.sin(colatitude)
    weights_lat = math.pi / NLAT * sine_lat
    synth_re, synth_im = solve_spectral(coef_re, coef_im, cosine_lat, sine_lat, weights_lat, orders)
    factor = jnp.where(orders == 0, jnp.float32(1.0), jnp.float32(2.0))
    potential = jnp.dot(synth_re * factor, cos_table.T, precision=HIGHEST_PRECISION) - jnp.dot(synth_im * factor, sin_table.T, precision=HIGHEST_PRECISION)
    shell_potential = jnp.take(potential.reshape(-1), flat_cells)
    return (parallel_flow_charge, fac_grid, potential, shell_potential)
```

```python
import functools
import math

import jax
import jax.numpy as jnp
from jax import lax
from jax.experimental import pallas as pl
from jax.experimental.pallas import tpu as pltpu
from jax.sharding import PartitionSpec as P

LEVELS = 4
STEPS = 2
LAT_DEV = 2
NLON = 1024
DEGREES = 512


COURANT = 0.3
KAPPA2 = 400.0
POT_GAIN = 2000.0
HIGHEST_PRECISION = lax.Precision.HIGHEST


def passed_along(value, axis, steps):
    count = lax.axis_size(axis)
    leading, last = (max(0, -steps), min(count, count - steps))
    return lax.ppermute(value, axis, [(source, source + steps) for source in range(leading, last)])


def iota(shape, dim):
    return lax.broadcasted_iota(jnp.int32, shape, dim)


def face_selection():
    cell, col = iota((512, 256), 0), iota((512, 256), 1)
    face, c = col // 64, col % 64
    along_y = 64 * (c // 8) + jnp.where(face == 0, 56, 0) + c % 8
    along_z = 64 * (c // 8) + 8 * (c % 8) + jnp.where(face == 2, 7, 0)
    return (cell == jnp.where(face < 2, along_y, along_z)).astype(jnp.bfloat16)


def ghost_expansion():
    shape = (2, 256, 512)
    along, row, cell = iota(shape, 0), iota(shape, 1) % 128, iota(shape, 2)
    c, top = row % 64, row // 64
    target_y = 64 * (c // 8) + 56 * top + c % 8
    target_z = 64 * (c // 8) + 8 * (c % 8) + 7 * top
    return (cell == jnp.where(along == 0, target_y, target_z)).astype(jnp.bfloat16)


def patch_selection():
    cell, k = iota((512, 128), 0), iota((512, 128), 1)
    return (cell == 8 * (k % 64) + k // 64).astype(jnp.bfloat16)


def split_two(value):
    high = value.astype(jnp.bfloat16)
    return high, (value - high.astype(jnp.float32)).astype(jnp.bfloat16)


def product(left, right):
    return jnp.dot(left, right, preferred_element_type=jnp.float32)


def write_faces(state_ref, select_ref, faces_ref):
    first_half = iota((64, 128), 1) < 64
    selection = select_ref[...]
    for v in range(state_ref.shape[0]):
        head = pltpu.roll(state_ref[v, :, 0:128], 64, 1)
        tail = pltpu.roll(state_ref[v, :, 384:512], 64, 1)
        faces_ref[v, :, 0:128] = jnp.where(first_half, tail, head)
        high, low = split_two(state_ref[v])
        faces_ref[v, :, 128:384] = product(high, selection) + product(low, selection)


def faces_kernel(state_ref, select_ref, faces_ref):
    write_faces(state_ref, select_ref, faces_ref)


def step_kernel(
    mix_ref,
    speed_ref,
    flow_ref,
    state_ref,
    prev_ref,
    own_ref,
    next_ref,
    pick_ref,
    expand_ref,
    rate_ref,
    select_ref,
    out_ref,
    extra_ref,
    ghost_ref,
    spread_ref,
    gx_ref,
    last,
):
    variables = state_ref.shape[0]
    first_half = iota((64, 128), 1) < 64
    for d in range(3):
        lanes = slice(128 * d, 128 * d + 128)
        for v in range(variables):
            own = own_ref[v, :, lanes]
            table = jnp.concatenate(
                [prev_ref[v, :, lanes], own, next_ref[v, :, lanes], pltpu.roll(own, 64, 1)], axis=0
            )
            both = product(pick_ref[d], jnp.concatenate(split_two(table), axis=1))
            high = jnp.where(first_half, both[0:64, 0:128], both[64:128, 0:128])
            low = jnp.where(first_half, both[0:64, 128:256], both[64:128, 128:256])
            if d == 0:
                gx_ref[v] = high + low
            else:
                ghost_ref[d - 1, pl.ds(64 * v, 64), 0:128] = high.astype(jnp.bfloat16)
                ghost_ref[d - 1, pl.ds(64 * v, 64), 128:256] = low.astype(jnp.bfloat16)
    for d in range(2):
        spread_ref[d] = product(ghost_ref[d], expand_ref[d])

    lane = iota((8, 128), 1)
    lower_half = lane < 64
    y_low, y_top = lane // 8 % 8 == 0, lane // 8 % 8 == 7
    z_low, z_top = lane % 8 == 0, lane % 8 == 7

    def rows_step(group, carry):
        start = pl.multiple_of(8 * group, 8)
        rows = pl.ds(start, 8)
        rate = rate_ref[rows, :]
        for chunk in range(4):
            lanes = slice(128 * chunk, 128 * chunk + 128)
            diffs, values, smooth = [[], [], []], [], []
            for v in range(variables):
                u = state_ref[v, rows, lanes]
                middle = pltpu.roll(u, 64, 1)
                if chunk > 0:
                    below = pltpu.roll(state_ref[v, rows, 128 * chunk - 128 : 128 * chunk], 64, 1)
                else:
                    below = gx_ref[v, rows, :]
                if chunk < 3:
                    above = pltpu.roll(state_ref[v, rows, 128 * chunk + 128 : 128 * chunk + 256], 64, 1)
                else:
                    above = gx_ref[v, rows, :]
                spread_rows = pl.ds(pl.multiple_of(64 * v + start, 8), 8)
                gy = spread_ref[0, spread_rows, lanes]
                gz = spread_ref[1, spread_rows, lanes]
                pairs = [
                    (jnp.where(lower_half, below, middle), jnp.where(lower_half, middle, above)),
                    (
                        jnp.where(y_low, gy, pltpu.roll(u, 8, 1)),
                        jnp.where(y_top, gy, pltpu.roll(u, 120, 1)),
                    ),
                    (
                        jnp.where(z_low, gz, pltpu.roll(u, 1, 1)),
                        jnp.where(z_top, gz, pltpu.roll(u, 127, 1)),
                    ),
                ]
                twice = u + u
                total = None
                for d in range(3):
                    lower, upper = pairs[d]
                    diffs[d].append(upper - lower)
                    term = speed_ref[d] * ((upper - twice) + lower)
                    total = term if total is None else total + term
                values.append(u)
                smooth.append(total)
            for i in range(variables):
                change = -smooth[i]
                for d in range(3):
                    for j in range(variables):
                        change = change + mix_ref[64 * d + 8 * i + j] * diffs[d][j]
                out_ref[i, rows, lanes] = values[i] - rate * change
        return carry

    lax.fori_loop(0, 8, rows_step, 0)
    if last:
        total = flow_ref[0] * out_ref[0]
        for v in range(1, variables):
            total = total + flow_ref[v] * out_ref[v]
        high, rest = total.astype(jnp.bfloat16), None
        rest = total - high.astype(jnp.float32)
        middle, low = split_two(rest)
        selection = select_ref[...]
        extra_ref[...] = product(high, selection) + (
            product(middle, selection) + product(low, selection)
        )
    else:
        write_faces(out_ref, select_ref, extra_ref)


SMEM_SPEC = pl.BlockSpec(memory_space=pltpu.SMEM)
VMEM_SPEC = pl.BlockSpec(memory_space=pltpu.VMEM)
INTERPRET = False


def make_faces(state_in, selection):
    return pl.pallas_call(
        faces_kernel,
        out_shape=jax.ShapeDtypeStruct(state_in.shape[:2] + (384,), jnp.float32),
        in_specs=[VMEM_SPEC] * 2,
        out_specs=VMEM_SPEC,
        interpret=INTERPRET,
    )(state_in, selection)


def advance(mix, speeds, flow, state_in, prev, own, following, pick, expand, rate, selection, last):
    variables, blocks = state_in.shape[:2]
    extra = (blocks, 128) if last else (variables, blocks, 384)
    return pl.pallas_call(
        functools.partial(step_kernel, last=last),
        out_shape=(
            jax.ShapeDtypeStruct(state_in.shape, jnp.float32),
            jax.ShapeDtypeStruct(extra, jnp.float32),
        ),
        in_specs=[SMEM_SPEC] * 3 + [VMEM_SPEC] * 8,
        out_specs=(VMEM_SPEC, VMEM_SPEC),
        scratch_shapes=[
            pltpu.VMEM((2, 64 * variables, 256), jnp.bfloat16),
            pltpu.VMEM((2, 64 * variables, 512), jnp.float32),
            pltpu.VMEM((variables, 64, 128), jnp.float32),
        ],
        interpret=INTERPRET,
    )(mix, speeds, flow, state_in, prev, own, following, pick, expand, rate, selection)


def block_picks(neighbours, offset):
    blocks = neighbours.shape[0]
    local = jnp.where(
        neighbours >= 0, neighbours - offset, 3 * blocks + jnp.arange(blocks, dtype=jnp.int32)[:, None]
    )
    index = jnp.transpose(local).reshape(3, 2 * blocks)
    return (index[:, :, None] == iota((3, 2 * blocks, 4 * blocks), 2)).astype(jnp.bfloat16)


def wave_speeds(flux_derivative_matrices):
    return jnp.max(jnp.sum(jnp.abs(flux_derivative_matrices), axis=2), axis=1)


def fourier_tables(orders):
    longitudes = jnp.arange(NLON, dtype=jnp.int32)
    phase_index = longitudes[:, None] * orders[None, :] % NLON
    angle_rad = phase_index.astype(jnp.float32) * (2.0 * math.pi / NLON)
    return (jnp.cos(angle_rad), jnp.sin(angle_rad))


def legendre_start(sine_lat, orders):
    series_k = jnp.arange(1, DEGREES, dtype=jnp.int32).astype(jnp.float32)
    log_sums = jnp.concatenate(
        [
            jnp.zeros((1,), jnp.float32),
            jnp.cumsum(0.5 * jnp.log((2.0 * series_k + 1.0) / (2.0 * series_k))),
        ]
    )
    log_base = jnp.take(log_sums, orders)
    order_real = orders.astype(jnp.float32)
    return jnp.exp(
        0.5 * math.log(0.5) + log_base[None, :] + order_real[None, :] * jnp.log(sine_lat)[:, None]
    )


def recurrence_factors(orders):
    degree = iota((DEGREES, orders.shape[0]), 0)
    order = jnp.broadcast_to(orders[None, :], degree.shape)
    degree_real, order_real = degree.astype(jnp.float32), order.astype(jnp.float32)
    ratio_up = jnp.sqrt(
        jnp.maximum(4.0 * degree_real * degree_real - 1.0, 1.0)
        / jnp.maximum(degree_real * degree_real - order_real * order_real, 1.0)
    )
    lower_deg = degree_real - 1.0
    ratio_back = jnp.sqrt(
        jnp.maximum(lower_deg * lower_deg - order_real * order_real, 0.0)
        / jnp.maximum(4.0 * lower_deg * lower_deg - 1.0, 1.0)
    )
    coef_prev = jnp.where(
        degree == order + 1,
        jnp.sqrt(2.0 * order_real + 3.0),
        jnp.where(degree >= order + 2, ratio_up, 0.0),
    )
    coef_before = jnp.where(degree >= order + 2, -ratio_up * ratio_back, 0.0)
    return coef_prev, coef_before


def spectral_kernel(
    first_ref, prev_ref, before_ref, gain_ref, re_ref, im_ref, diagonal_ref, cosine_ref, out_re, out_im
):
    even = iota((8, 128), 0) % 2 == 0
    order = first_ref[0] + iota((8, 128), 0) % 2
    rows_re, rows_im = re_ref[...], im_ref[...]
    diagonal, cosine = diagonal_ref[...], cosine_ref[...]
    zero = jnp.zeros((8, 128), jnp.float32)

    def over_latitudes(value):
        value = value + pltpu.roll(value, 4, 0)
        value = value + pltpu.roll(value, 2, 0)
        return jnp.sum(value, axis=1, keepdims=True)

    def some_degrees(step, carried):
        previous, before, acc_re, acc_im = carried
        for inner in range(16):
            degree = 16 * step + inner
            up = jnp.where(even, prev_ref[2 * degree], prev_ref[2 * degree + 1])
            back = jnp.where(even, before_ref[2 * degree], before_ref[2 * degree + 1])
            present = (up * cosine) * previous + back * before
            present = jnp.where(order == degree, diagonal, present)
            gain = gain_ref[degree]
            acc_re = acc_re + (gain * over_latitudes(rows_re * present)) * present
            acc_im = acc_im + (gain * over_latitudes(rows_im * present)) * present
            previous, before = present, previous
        return previous, before, acc_re, acc_im

    carried = lax.fori_loop(0, DEGREES // 16, some_degrees, (zero, zero, zero, zero))
    out_re[...] = carried[2]
    out_im[...] = carried[3]


def solve_spectral(coef_re, coef_im, cosine_lat, sine_lat, weights_lat, orders):
    def folded(rows):
        return jnp.swapaxes(rows.reshape(2, 4, 128), 0, 1).reshape(8, 128)

    def unfolded(value):
        return jnp.swapaxes(value.reshape(4, 2, 128), 0, 1).reshape(2, 512)

    diagonal = folded(jnp.transpose(legendre_start(sine_lat, orders)))
    coef_prev, coef_before = recurrence_factors(orders)
    degree_real = jnp.arange(DEGREES, dtype=jnp.int32).astype(jnp.float32)
    gain = POT_GAIN / (degree_real * (degree_real + 1.0) + KAPPA2)
    shape = jax.ShapeDtypeStruct((8, 128), jnp.float32)
    acc_re, acc_im = pl.pallas_call(
        spectral_kernel,
        out_shape=(shape, shape),
        in_specs=[SMEM_SPEC] * 4 + [VMEM_SPEC] * 4,
        out_specs=(VMEM_SPEC, VMEM_SPEC),
        interpret=INTERPRET,
    )(
        orders[0:1],
        coef_prev.reshape(-1),
        coef_before.reshape(-1),
        gain,
        folded(coef_re * weights_lat[None, :]),
        folded(coef_im * weights_lat[None, :]),
        diagonal,
        folded(jnp.broadcast_to(cosine_lat[None, :], (2, 512))),
    )
    return unfolded(acc_re), unfolded(acc_im)


def body(
    invariant_fluid_quantities,
    flux_derivative_matrices,
    levels,
    neighbours,
    block_latitude_band,
    block_longitude_segment,
    parallel_flow_coefficients,
):
    grp_size = lax.axis_size("grp")
    core_size = lax.axis_size("cores")
    device_total = grp_size * core_size
    block_portion = invariant_fluid_quantities.shape[1]
    state_variables = invariant_fluid_quantities.shape[0]
    device = lax.axis_index(("grp", "cores"))
    speeds = wave_speeds(flux_derivative_matrices)
    rate_block = COURANT * jnp.exp2(levels.astype(jnp.float32) - (LEVELS - 1)) / jnp.max(speeds)
    offset = (device - 1) * block_portion
    picks = block_picks(neighbours, offset)
    selection, expand = face_selection(), ghost_expansion()
    rate = jnp.broadcast_to(rate_block[:, None], (block_portion, 128))
    mix = 0.5 * flux_derivative_matrices.reshape(-1)
    half_speeds = 0.5 * speeds
    parallel_flow_charge = invariant_fluid_quantities
    faces = make_faces(parallel_flow_charge, selection)
    for section_index in range(STEPS):
        last = section_index == STEPS - 1
        parallel_flow_charge, faces = advance(
            mix,
            half_speeds,
            parallel_flow_coefficients,
            parallel_flow_charge,
            passed_along(faces, ("grp", "cores"), 1),
            faces,
            passed_along(faces, ("grp", "cores"), -1),
            picks,
            expand,
            rate,
            patch_selection() if last else selection,
            last,
        )
    patches = faces
    band_index = block_latitude_band[:, 0]
    block_ids = jnp.arange(block_portion, dtype=jnp.int32)
    earlier = (band_index[None, :] == band_index[:, None]) & (
        block_ids[None, :] < block_ids[:, None]
    )
    rank_in_band = jnp.sum(earlier.astype(jnp.int32), axis=1)
    capacity = max(2, 2 * block_portion // grp_size)
    slot_index = band_index * capacity + rank_in_band
    slot_ids = jnp.arange(grp_size * capacity, dtype=jnp.int32)
    placing = (slot_ids[:, None] == slot_index[None, :]).astype(jnp.float32)
    send_rows = jnp.dot(placing, patches, precision=HIGHEST_PRECISION).reshape(
        grp_size, capacity, 128
    )
    send_codes = jnp.dot(
        placing, (block_longitude_segment + 1).astype(jnp.float32), precision=HIGHEST_PRECISION
    ).reshape(grp_size, capacity)
    got_rows, got_codes = (
        lax.all_to_all(send_rows, "grp", split_axis=0, concat_axis=0, tiled=True),
        lax.all_to_all(send_codes, "grp", split_axis=0, concat_axis=0, tiled=True),
    )
    segments = NLON // 64
    segment_codes = jnp.arange(1, segments + 1, dtype=jnp.int32).astype(jnp.float32)
    landing = (got_codes.reshape(-1)[:, None] == segment_codes[None, :]).astype(jnp.float32)
    gathered = jnp.dot(landing.T, got_rows.reshape(-1, 128), precision=HIGHEST_PRECISION)
    fac_local = jnp.swapaxes(gathered.reshape(segments, LAT_DEV, 64), 0, 1).reshape(LAT_DEV, NLON)
    orders_all = jnp.arange(DEGREES, dtype=jnp.int32)
    cos_table, sin_table = fourier_tables(orders_all)
    coef_re = jnp.dot(fac_local, cos_table, precision=HIGHEST_PRECISION) / NLON
    coef_im = -jnp.dot(fac_local, sin_table, precision=HIGHEST_PRECISION) / NLON
    lat_total = LAT_DEV * device_total
    degree_share = DEGREES // device_total
    lat_ids = jnp.arange(lat_total, dtype=jnp.int32)
    colatitude = (lat_ids.astype(jnp.float32) + 0.5) * (math.pi / lat_total)
    cosine_all = jnp.cos(colatitude)
    sine_all = jnp.sin(colatitude)
    weights_all = math.pi / lat_total * sine_all
    own_orders = device * degree_share + jnp.arange(degree_share, dtype=jnp.int32)
    stacked = jnp.stack([coef_re, coef_im])
    regrouped = lax.all_to_all(
        lax.all_to_all(stacked, "grp", split_axis=2, concat_axis=1, tiled=True),
        "cores",
        split_axis=2,
        concat_axis=1,
        tiled=True,
    )
    regrouped = jnp.transpose(
        regrouped.reshape(2, core_size, grp_size, LAT_DEV, degree_share), (0, 2, 1, 3, 4)
    ).reshape(2, lat_total, degree_share)
    synth_re, synth_im = solve_spectral(
        jnp.transpose(regrouped[0]),
        jnp.transpose(regrouped[1]),
        cosine_all,
        sine_all,
        weights_all,
        own_orders,
    )
    synth_both = jnp.stack([jnp.transpose(synth_re), jnp.transpose(synth_im)])
    returned = lax.all_to_all(
        lax.all_to_all(synth_both, "grp", split_axis=1, concat_axis=2, tiled=True),
        "cores",
        split_axis=1,
        concat_axis=2,
        tiled=True,
    )
    column_ids = jnp.arange(DEGREES, dtype=jnp.int32)
    order_perm = (
        degree_share
        * (
            core_size * (column_ids // degree_share % grp_size)
            + column_ids // (grp_size * degree_share)
        )
        + column_ids % degree_share
    )
    cos_perm, sin_perm = fourier_tables(order_perm)
    factor = jnp.where(order_perm == 0, jnp.float32(1.0), jnp.float32(2.0))
    potential_local = jnp.dot(
        returned[0] * factor, cos_perm.T, precision=HIGHEST_PRECISION
    ) - jnp.dot(returned[1] * factor, sin_perm.T, precision=HIGHEST_PRECISION)
    grid_segments = jnp.swapaxes(potential_local.reshape(LAT_DEV, segments, 64), 0, 1).reshape(
        segments, 128
    )
    back_rows = jnp.dot(landing, grid_segments, precision=HIGHEST_PRECISION).reshape(
        grp_size, capacity, 128
    )
    home_rows = lax.all_to_all(back_rows, "grp", split_axis=0, concat_axis=0, tiled=True)
    shell_potential = jnp.dot(placing.T, home_rows.reshape(-1, 128), precision=HIGHEST_PRECISION)
    return (parallel_flow_charge, fac_local, potential_local, shell_potential)


def solution(mesh):
    placed = (
        P(None, ("grp", "cores"), None),
        P(),
        P(("grp", "cores")),
        P(("grp", "cores"), None),
        P(("grp", "cores"), None),
        P(("grp", "cores")),
        P(),
    )
    return jax.shard_map(
        body,
        mesh=mesh,
        in_specs=placed,
        out_specs=(
            P(None, ("grp", "cores"), None),
            P(("grp", "cores"), None),
            P(("grp", "cores"), None),
            P(("grp", "cores"), None),
        ),
        check_vma=False,
    )
```

```python
import functools
import math

import jax
import jax.numpy as jnp
import numpy as np
from jax import lax
from jax.experimental import pallas as pl
from jax.experimental.pallas import tpu as pltpu
from jax.sharding import PartitionSpec as P

LEVELS = 4
STEPS = 2
LAT_DEV = 2
NLON = 1024
DEGREES = 512


COURANT = 0.3
KAPPA2 = 400.0
POT_GAIN = 2000.0
HIGHEST_PRECISION = lax.Precision.HIGHEST


def passed_along(value, axis, steps):
    count = lax.axis_size(axis)
    leading, last = (max(0, -steps), min(count, count - steps))
    return lax.ppermute(value, axis, [(source, source + steps) for source in range(leading, last)])


def iota(shape, dim):
    return lax.broadcasted_iota(jnp.int32, shape, dim)


def face_selection():
    cell, col = iota((512, 256), 0), iota((512, 256), 1)
    face, c = col // 64, col % 64
    along_y = 64 * (c // 8) + jnp.where(face == 0, 56, 0) + c % 8
    along_z = 64 * (c // 8) + 8 * (c % 8) + jnp.where(face == 2, 7, 0)
    return (cell == jnp.where(face < 2, along_y, along_z)).astype(jnp.bfloat16)


def ghost_expansion():
    shape = (2, 256, 512)
    along, row, cell = iota(shape, 0), iota(shape, 1) % 128, iota(shape, 2)
    c, top = row % 64, row // 64
    target_y = 64 * (c // 8) + 56 * top + c % 8
    target_z = 64 * (c // 8) + 8 * (c % 8) + 7 * top
    return (cell == jnp.where(along == 0, target_y, target_z)).astype(jnp.bfloat16)


def patch_selection():
    cell, k = iota((512, 128), 0), iota((512, 128), 1)
    return (cell == 8 * (k % 64) + k // 64).astype(jnp.bfloat16)


def split_two(value):
    high = value.astype(jnp.bfloat16)
    return high, (value - high.astype(jnp.float32)).astype(jnp.bfloat16)


def split_three(value):
    high = value.astype(jnp.bfloat16)
    return (high,) + split_two(value - high.astype(jnp.float32))


def sum_of_parts(parts):
    return parts[0] + (parts[1] + parts[2])


def product_of_parts(parts, right):
    return [product(part, right) for part in parts]


def exact(left, right, left_dim=1, right_dim=0):
    return lax.dot_general(
        left,
        right,
        (((left_dim,), (right_dim,)), ((), ())),
        precision=HIGHEST_PRECISION,
        preferred_element_type=jnp.float32,
    )


def product(left, right):
    return jnp.dot(left, right, preferred_element_type=jnp.float32)


def write_faces(state_ref, select_ref, faces_ref):
    first_half = iota((64, 128), 1) < 64
    selection = select_ref[...]
    for v in range(state_ref.shape[0]):
        head = pltpu.roll(state_ref[v, :, 0:128], 64, 1)
        tail = pltpu.roll(state_ref[v, :, 384:512], 64, 1)
        faces_ref[v, :, 0:128] = jnp.where(first_half, tail, head)
        high, low = split_two(state_ref[v])
        faces_ref[v, :, 128:384] = product(high, selection) + product(low, selection)


def faces_kernel(state_ref, select_ref, faces_ref):
    write_faces(state_ref, select_ref, faces_ref)


def step_kernel(
    mix_ref,
    speed_ref,
    flow_ref,
    state_ref,
    prev_ref,
    own_ref,
    next_ref,
    pick_ref,
    expand_ref,
    rate_ref,
    select_ref,
    place_ref,
    segment_ref,
    out_ref,
    extra_ref,
    ghost_ref,
    spread_ref,
    gx_ref,
    last,
):
    variables = state_ref.shape[0]
    first_half = iota((64, 128), 1) < 64
    for d in range(3):
        lanes = slice(128 * d, 128 * d + 128)
        for v in range(variables):
            own = own_ref[v, :, lanes]
            table = jnp.concatenate(
                [prev_ref[v, :, lanes], own, next_ref[v, :, lanes], pltpu.roll(own, 64, 1)], axis=0
            )
            both = product(pick_ref[d], jnp.concatenate(split_two(table), axis=1))
            high = jnp.where(first_half, both[0:64, 0:128], both[64:128, 0:128])
            low = jnp.where(first_half, both[0:64, 128:256], both[64:128, 128:256])
            if d == 0:
                gx_ref[v] = high + low
            else:
                ghost_ref[d - 1, pl.ds(64 * v, 64), 0:128] = high.astype(jnp.bfloat16)
                ghost_ref[d - 1, pl.ds(64 * v, 64), 128:256] = low.astype(jnp.bfloat16)
    for d in range(2):
        spread_ref[d] = product(ghost_ref[d], expand_ref[d])

    lane = iota((8, 128), 1)
    lower_half = lane < 64
    y_low, y_top = lane // 8 % 8 == 0, lane // 8 % 8 == 7
    z_low, z_top = lane % 8 == 0, lane % 8 == 7

    def rows_step(group, carry):
        start = pl.multiple_of(8 * group, 8)
        rows = pl.ds(start, 8)
        rate = rate_ref[rows, :]
        for chunk in range(4):
            lanes = slice(128 * chunk, 128 * chunk + 128)
            diffs, values, smooth = [[], [], []], [], []
            for v in range(variables):
                u = state_ref[v, rows, lanes]
                middle = pltpu.roll(u, 64, 1)
                if chunk > 0:
                    below = pltpu.roll(state_ref[v, rows, 128 * chunk - 128 : 128 * chunk], 64, 1)
                else:
                    below = gx_ref[v, rows, :]
                if chunk < 3:
                    above = pltpu.roll(state_ref[v, rows, 128 * chunk + 128 : 128 * chunk + 256], 64, 1)
                else:
                    above = gx_ref[v, rows, :]
                spread_rows = pl.ds(pl.multiple_of(64 * v + start, 8), 8)
                gy = spread_ref[0, spread_rows, lanes]
                gz = spread_ref[1, spread_rows, lanes]
                pairs = [
                    (jnp.where(lower_half, below, middle), jnp.where(lower_half, middle, above)),
                    (
                        jnp.where(y_low, gy, pltpu.roll(u, 8, 1)),
                        jnp.where(y_top, gy, pltpu.roll(u, 120, 1)),
                    ),
                    (
                        jnp.where(z_low, gz, pltpu.roll(u, 1, 1)),
                        jnp.where(z_top, gz, pltpu.roll(u, 127, 1)),
                    ),
                ]
                twice = u + u
                total = None
                for d in range(3):
                    lower, upper = pairs[d]
                    diffs[d].append(upper - lower)
                    term = speed_ref[d] * ((upper - twice) + lower)
                    total = term if total is None else total + term
                values.append(u)
                smooth.append(total)
            for i in range(variables):
                change = -smooth[i]
                for d in range(3):
                    for j in range(variables):
                        change = change + mix_ref[64 * d + 8 * i + j] * diffs[d][j]
                out_ref[i, rows, lanes] = values[i] - rate * change
        return carry

    lax.fori_loop(0, 8, rows_step, 0)
    if last:
        total = flow_ref[0] * out_ref[0]
        for v in range(1, variables):
            total = total + flow_ref[v] * out_ref[v]
        patches = sum_of_parts(product_of_parts(split_three(total), select_ref[...]))
        parts = jnp.concatenate(split_three(patches) + (segment_ref[...],), axis=1)
        sent = [product(place_ref[0], parts), product(place_ref[1], parts)]
        for k in range(2):
            extra_ref[:, 128 * k : 128 * k + 128] = sum_of_parts(
                [sent[k][:, 128 * i : 128 * i + 128] for i in range(3)]
            )
        extra_ref[:, 256:384] = jnp.where(
            iota((128, 128), 1) < 64, sent[0][:, 384:512], sent[1][:, 384:512]
        )
    else:
        write_faces(out_ref, select_ref, extra_ref)


SMEM_SPEC = pl.BlockSpec(memory_space=pltpu.SMEM)
VMEM_SPEC = pl.BlockSpec(memory_space=pltpu.VMEM)
INTERPRET = False


def make_faces(state_in, selection):
    return pl.pallas_call(
        faces_kernel,
        out_shape=jax.ShapeDtypeStruct(state_in.shape[:2] + (384,), jnp.float32),
        in_specs=[VMEM_SPEC] * 2,
        out_specs=VMEM_SPEC,
        interpret=INTERPRET,
    )(state_in, selection)


def advance(mix, speeds, flow, state_in, prev, own, following, pick, expand, rate, selection, place, segment, last):
    variables, blocks = state_in.shape[:2]
    extra = (128, 384) if last else (variables, blocks, 384)
    return pl.pallas_call(
        functools.partial(step_kernel, last=last),
        out_shape=(
            jax.ShapeDtypeStruct(state_in.shape, jnp.float32),
            jax.ShapeDtypeStruct(extra, jnp.float32),
        ),
        in_specs=[SMEM_SPEC] * 3 + [VMEM_SPEC] * 10,
        out_specs=(VMEM_SPEC, VMEM_SPEC),
        scratch_shapes=[
            pltpu.VMEM((2, 64 * variables, 256), jnp.bfloat16),
            pltpu.VMEM((2, 64 * variables, 512), jnp.float32),
            pltpu.VMEM((variables, 64, 128), jnp.float32),
        ],
        interpret=INTERPRET,
    )(mix, speeds, flow, state_in, prev, own, following, pick, expand, rate, selection, place, segment)


def block_picks(neighbours, offset):
    blocks = neighbours.shape[0]
    local = jnp.where(
        neighbours >= 0, neighbours - offset, 3 * blocks + jnp.arange(blocks, dtype=jnp.int32)[:, None]
    )
    index = jnp.transpose(local).reshape(3, 2 * blocks)
    return (index[:, :, None] == iota((3, 2 * blocks, 4 * blocks), 2)).astype(jnp.bfloat16)


def wave_speeds(flux_derivative_matrices):
    return jnp.max(jnp.sum(jnp.abs(flux_derivative_matrices), axis=2), axis=1)


def transform_tables():
    column = np.arange(64)
    q, imaginary = 2 * (column // 8) + column % 2, column // 4 % 2 == 1
    s, r, n = np.arange(16), np.arange(64), np.arange(32)
    step = 2.0 * np.pi * np.outer(s, q) / 16
    twist = 2.0 * np.pi * np.outer(r, q) / NLON
    wave = 2.0 * np.pi * np.outer(n, r) / 64
    split = np.concatenate([np.cos(step), -np.sin(step)], axis=1)
    twiddle = np.stack([np.cos(twist), np.sin(twist)])
    forward = np.concatenate([np.cos(wave), np.sin(wave)], axis=1) / NLON
    backward = np.concatenate([np.cos(wave), np.sin(wave)], axis=0).T
    factor = np.where((n[:, None] == 0) & (q[None, :] == 0), 1.0, 2.0)
    untwist = np.stack(
        [
            np.where(imaginary, -np.sin(twist), np.cos(twist)),
            np.where(imaginary, -np.cos(twist), -np.sin(twist)),
        ]
    )
    of_latitude = [(column // 2 % 2 == latitude)[None, :] for latitude in range(2)]
    join = np.concatenate(
        [np.concatenate([np.cos(step) * own, np.sin(step) * own], axis=1) for own in of_latitude]
    )
    return [
        jnp.asarray(table.astype(np.float32))
        for table in (split, twiddle, forward, factor, backward, untwist, join)
    ]


def landing_of(codes, k):
    return codes[:, 64 * k : 64 * k + 16] == (iota((128, 16), 1) + 1).astype(jnp.float32)


def forward_kernel(got_ref, split_ref, twiddle_ref, forward_ref, grid_ref, send_ref):
    grid = None
    codes = got_ref[:, 256:384]
    for k in range(2):
        landing = landing_of(codes, k).astype(jnp.float32)
        part = exact(landing, got_ref[:, 128 * k : 128 * k + 128], 0, 0)
        grid = part if grid is None else grid + part
    grid_ref[...] = grid
    column = iota((64, 64), 1)
    split = split_ref[...]
    first, second = exact(grid[:, 0:64], split, 0, 0), exact(grid[:, 64:128], split, 0, 0)
    of_first = column // 2 % 2 == 0
    even = jnp.where(of_first, first[:, 0:64], second[:, 0:64])
    odd = jnp.where(of_first, first[:, 64:128], second[:, 64:128])
    turned_re = even * twiddle_ref[0] + odd * twiddle_ref[1]
    turned_im = odd * twiddle_ref[0] - even * twiddle_ref[1]
    real = column // 4 % 2 == 0
    both = jnp.concatenate(
        [jnp.where(real, turned_re, turned_im), jnp.where(real, turned_im, -turned_re)], axis=0
    )
    coef = exact(forward_ref[...], both)
    for part in range(8):
        send_ref[32 * part : 32 * part + 32, :] = coef[:, 8 * part : 8 * part + 8]


def backward_kernel(
    synth_ref, got_ref, factor_ref, backward_ref, untwist_ref, join_ref, grid_ref, back_ref, pair_ref
):
    for part in range(8):
        columns = slice(8 * part, 8 * part + 8)
        values = synth_ref[32 * part : 32 * part + 32, :]
        pair_ref[0:32, columns] = values
        pair_ref[32:64, columns] = jnp.concatenate([-values[:, 4:8], values[:, 0:4]], axis=1)
    factor = factor_ref[...]
    pair = pair_ref[...] * jnp.concatenate([factor, factor], axis=0)
    rows = exact(backward_ref[...], pair)
    turned = jnp.concatenate([rows * untwist_ref[0], rows * untwist_ref[1]], axis=1)
    joined = exact(join_ref[...], turned, 1, 1)
    grid_ref[:, 0:64] = joined[0:16]
    grid_ref[:, 64:128] = joined[16:32]
    parts = jnp.concatenate(split_three(grid_ref[...]), axis=1)
    codes = got_ref[:, 256:384]
    for k in range(2):
        found = product(landing_of(codes, k).astype(jnp.float32).astype(jnp.bfloat16), parts)
        back_ref[:, 128 * k : 128 * k + 128] = sum_of_parts(
            [found[:, 128 * i : 128 * i + 128] for i in range(3)]
        )


def home_kernel(home_ref, place_ref, shell_ref):
    total = None
    for k in range(2):
        parts = jnp.concatenate(split_three(home_ref[:, 128 * k : 128 * k + 128]), axis=1)
        found = lax.dot_general(
            place_ref[k], parts, (((0,), (0,)), ((), ())), preferred_element_type=jnp.float32
        )
        part = sum_of_parts([found[:, 128 * i : 128 * i + 128] for i in range(3)])
        total = part if total is None else total + part
    shell_ref[...] = total


def run_kernel(kernel, operands, shapes, scratch=()):
    return pl.pallas_call(
        kernel,
        out_shape=tuple(jax.ShapeDtypeStruct(shape, jnp.float32) for shape in shapes),
        in_specs=[VMEM_SPEC] * len(operands),
        out_specs=tuple([VMEM_SPEC] * len(shapes)),
        scratch_shapes=[pltpu.VMEM(shape, jnp.float32) for shape in scratch],
        interpret=INTERPRET,
    )(*operands)


def legendre_start(sine_lat, orders):
    series_k = jnp.arange(1, DEGREES, dtype=jnp.int32).astype(jnp.float32)
    log_sums = jnp.concatenate(
        [
            jnp.zeros((1,), jnp.float32),
            jnp.cumsum(0.5 * jnp.log((2.0 * series_k + 1.0) / (2.0 * series_k))),
        ]
    )
    log_base = jnp.take(log_sums, orders)
    return jnp.exp(0.5 * math.log(0.5) + log_base + orders.astype(jnp.float32) * jnp.log(sine_lat))


def recurrence_factors(orders):
    degree = iota((DEGREES, orders.shape[0]), 0)
    order = jnp.broadcast_to(orders[None, :], degree.shape)
    degree_real, order_real = degree.astype(jnp.float32), order.astype(jnp.float32)
    ratio_up = jnp.sqrt(
        jnp.maximum(4.0 * degree_real * degree_real - 1.0, 1.0)
        / jnp.maximum(degree_real * degree_real - order_real * order_real, 1.0)
    )
    lower_deg = degree_real - 1.0
    ratio_back = jnp.sqrt(
        jnp.maximum(lower_deg * lower_deg - order_real * order_real, 0.0)
        / jnp.maximum(4.0 * lower_deg * lower_deg - 1.0, 1.0)
    )
    coef_prev = jnp.where(
        degree == order + 1,
        jnp.sqrt(2.0 * order_real + 3.0),
        jnp.where(degree >= order + 2, ratio_up, 0.0),
    )
    coef_before = jnp.where(degree >= order + 2, -ratio_up * ratio_back, 0.0)
    return coef_prev, coef_before


def spectral_kernel(
    first_ref, prev_ref, before_ref, gain_ref, re_ref, im_ref, diagonal_ref, cosine_ref, out_re, out_im
):
    even = iota((8, 128), 0) % 2 == 0
    order = first_ref[0] + iota((8, 128), 0) % 2
    rows_re, rows_im = re_ref[...], im_ref[...]
    diagonal, cosine = diagonal_ref[...], cosine_ref[...]
    zero = jnp.zeros((8, 128), jnp.float32)

    def over_latitudes(value):
        value = value + pltpu.roll(value, 4, 0)
        value = value + pltpu.roll(value, 2, 0)
        return jnp.sum(value, axis=1, keepdims=True)

    def some_degrees(step, carried):
        previous, before, acc_re, acc_im = carried
        for inner in range(16):
            degree = 16 * step + inner
            up = jnp.where(even, prev_ref[2 * degree], prev_ref[2 * degree + 1])
            back = jnp.where(even, before_ref[2 * degree], before_ref[2 * degree + 1])
            present = (up * cosine) * previous + back * before
            present = jnp.where(order == degree, diagonal, present)
            gain = gain_ref[degree]
            acc_re = acc_re + (gain * over_latitudes(rows_re * present)) * present
            acc_im = acc_im + (gain * over_latitudes(rows_im * present)) * present
            previous, before = present, previous
        return previous, before, acc_re, acc_im

    carried = lax.fori_loop(0, DEGREES // 16, some_degrees, (zero, zero, zero, zero))
    out_re[...] = carried[2]
    out_im[...] = carried[3]


def solve_spectral(received, first_order, lat_total):
    rows = received.reshape(2, 128, 2, 4).transpose(2, 0, 3, 1).reshape(2, 8, 128)
    row, lane = iota((8, 128), 0), iota((8, 128), 1)
    lat_ids = 256 * (row // 4) + 2 * lane + row // 2 % 2
    colatitude = (lat_ids.astype(jnp.float32) + 0.5) * (math.pi / lat_total)
    cosine, sine = jnp.cos(colatitude), jnp.sin(colatitude)
    weights = math.pi / lat_total * sine
    orders = first_order + jnp.arange(2, dtype=jnp.int32)
    diagonal = legendre_start(sine, jnp.broadcast_to(jnp.tile(orders, 4)[:, None], (8, 128)))
    coef_prev, coef_before = recurrence_factors(orders)
    degree_real = jnp.arange(DEGREES, dtype=jnp.int32).astype(jnp.float32)
    gain = POT_GAIN / (degree_real * (degree_real + 1.0) + KAPPA2)
    shape = jax.ShapeDtypeStruct((8, 128), jnp.float32)
    acc_re, acc_im = pl.pallas_call(
        spectral_kernel,
        out_shape=(shape, shape),
        in_specs=[SMEM_SPEC] * 4 + [VMEM_SPEC] * 4,
        out_specs=(VMEM_SPEC, VMEM_SPEC),
        interpret=INTERPRET,
    )(
        orders[0:1],
        coef_prev.reshape(-1),
        coef_before.reshape(-1),
        gain,
        rows[0] * weights,
        rows[1] * weights,
        diagonal,
        cosine,
    )
    both = jnp.stack([acc_re, acc_im]).reshape(2, 2, 4, 128)
    return both.transpose(1, 3, 0, 2).reshape(256, 8)


def body(
    invariant_fluid_quantities,
    flux_derivative_matrices,
    levels,
    neighbours,
    block_latitude_band,
    block_longitude_segment,
    parallel_flow_coefficients,
):
    grp_size = lax.axis_size("grp")
    core_size = lax.axis_size("cores")
    device_total = grp_size * core_size
    block_portion = invariant_fluid_quantities.shape[1]
    state_variables = invariant_fluid_quantities.shape[0]
    device = lax.axis_index(("grp", "cores"))
    speeds = wave_speeds(flux_derivative_matrices)
    rate_block = COURANT * jnp.exp2(levels.astype(jnp.float32) - (LEVELS - 1)) / jnp.max(speeds)
    offset = (device - 1) * block_portion
    picks = block_picks(neighbours, offset)
    selection, expand = face_selection(), ghost_expansion()
    rate = jnp.broadcast_to(rate_block[:, None], (block_portion, 128))
    mix = 0.5 * flux_derivative_matrices.reshape(-1)
    half_speeds = 0.5 * speeds
    band_index = block_latitude_band[:, 0]
    block_ids = jnp.arange(block_portion, dtype=jnp.int32)
    earlier = (band_index[None, :] == band_index[:, None]) & (
        block_ids[None, :] < block_ids[:, None]
    )
    rank_in_band = jnp.sum(earlier.astype(jnp.int32), axis=1)
    shape = (2, grp_size, block_portion)
    place = (
        (band_index[None, None, :] == iota(shape, 1)) & (rank_in_band[None, None, :] == iota(shape, 0))
    ).astype(jnp.bfloat16)
    segment = jnp.broadcast_to(
        (block_longitude_segment + 1).astype(jnp.bfloat16)[:, None], (block_portion, 128)
    )
    parallel_flow_charge = invariant_fluid_quantities
    faces = make_faces(parallel_flow_charge, selection)
    for section_index in range(STEPS):
        last = section_index == STEPS - 1
        parallel_flow_charge, faces = advance(
            mix,
            half_speeds,
            parallel_flow_coefficients,
            parallel_flow_charge,
            passed_along(faces, ("grp", "cores"), 1),
            faces,
            passed_along(faces, ("grp", "cores"), -1),
            picks,
            expand,
            rate,
            patch_selection() if last else selection,
            place,
            segment,
            last,
        )
    split, twiddle, forward, factor, backward, untwist, join = transform_tables()
    got = lax.all_to_all(faces, "grp", split_axis=0, concat_axis=0, tiled=True)
    fac_segments, coef = run_kernel(
        forward_kernel, (got, split, twiddle, forward), ((16, 128), (device_total, 8))
    )
    axes = ("grp", "cores")
    received = lax.all_to_all(coef, axes, split_axis=0, concat_axis=0, tiled=True)
    synth = solve_spectral(received, 16 * (device % 32) + 2 * (device // 32), LAT_DEV * device_total)
    returned = lax.all_to_all(synth, axes, split_axis=0, concat_axis=0, tiled=True)
    grid_segments, back = run_kernel(
        backward_kernel,
        (returned, got, factor, backward, untwist, join),
        ((16, 128), (grp_size, 256)),
        scratch=((64, 64),),
    )
    home = lax.all_to_all(back, "grp", split_axis=0, concat_axis=0, tiled=True)
    (shell_potential,) = run_kernel(home_kernel, (home, place), ((block_portion, 128),))
    fac_local, potential_local = (
        jnp.swapaxes(grid.reshape(16, LAT_DEV, 64), 0, 1).reshape(LAT_DEV, NLON)
        for grid in (fac_segments, grid_segments)
    )
    return (parallel_flow_charge, fac_local, potential_local, shell_potential)


def solution(mesh):
    placed = (
        P(None, ("grp", "cores"), None),
        P(),
        P(("grp", "cores")),
        P(("grp", "cores"), None),
        P(("grp", "cores"), None),
        P(("grp", "cores")),
        P(),
    )
    return jax.shard_map(
        body,
        mesh=mesh,
        in_specs=placed,
        out_specs=(
            P(None, ("grp", "cores"), None),
            P(("grp", "cores"), None),
            P(("grp", "cores"), None),
            P(("grp", "cores"), None),
        ),
        check_vma=False,
    )
```

```python
import functools
import math

import jax
import jax.numpy as jnp
import numpy as np
from jax import lax
from jax.experimental import pallas as pl
from jax.experimental.pallas import tpu as pltpu
from jax.sharding import PartitionSpec as P

LEVELS = 4
STEPS = 2
LAT_DEV = 2
NLON = 1024
DEGREES = 512


COURANT = 0.3
KAPPA2 = 400.0
POT_GAIN = 2000.0
HIGHEST_PRECISION = lax.Precision.HIGHEST


def passed_along(value, axis, steps):
    count = lax.axis_size(axis)
    leading, last = (max(0, -steps), min(count, count - steps))
    return lax.ppermute(value, axis, [(source, source + steps) for source in range(leading, last)])


def iota(shape, dim):
    return lax.broadcasted_iota(jnp.int32, shape, dim)


def face_selection():
    cell, col = iota((512, 256), 0), iota((512, 256), 1)
    face, c = col // 64, col % 64
    along_y = 64 * (c // 8) + jnp.where(face == 0, 56, 0) + c % 8
    along_z = 64 * (c // 8) + 8 * (c % 8) + jnp.where(face == 2, 7, 0)
    return (cell == jnp.where(face < 2, along_y, along_z)).astype(jnp.bfloat16)


def ghost_expansion():
    shape = (2, 256, 512)
    along, row, cell = iota(shape, 0), iota(shape, 1) % 128, iota(shape, 2)
    c, top = row % 64, row // 64
    target_y = 64 * (c // 8) + 56 * top + c % 8
    target_z = 64 * (c // 8) + 8 * (c % 8) + 7 * top
    return (cell == jnp.where(along == 0, target_y, target_z)).astype(jnp.bfloat16)


def patch_selection():
    cell, k = iota((512, 128), 0), iota((512, 128), 1)
    return (cell == 8 * (k % 64) + k // 64).astype(jnp.bfloat16)


def split_two(value):
    high = value.astype(jnp.bfloat16)
    return high, (value - high.astype(jnp.float32)).astype(jnp.bfloat16)


def split_three(value):
    high = value.astype(jnp.bfloat16)
    return (high,) + split_two(value - high.astype(jnp.float32))


def sum_of_parts(parts):
    return parts[0] + (parts[1] + parts[2])


def product_of_parts(parts, right):
    return [product(part, right) for part in parts]


def exact(left, right, left_dim=1, right_dim=0):
    return lax.dot_general(
        left,
        right,
        (((left_dim,), (right_dim,)), ((), ())),
        precision=HIGHEST_PRECISION,
        preferred_element_type=jnp.float32,
    )


def product(left, right):
    return jnp.dot(left, right, preferred_element_type=jnp.float32)


def write_faces(state_ref, select_ref, faces_ref):
    first_half = iota((64, 128), 1) < 64
    selection = select_ref[...]
    for v in range(state_ref.shape[0]):
        head = pltpu.roll(state_ref[v, :, 0:128], 64, 1)
        tail = pltpu.roll(state_ref[v, :, 384:512], 64, 1)
        faces_ref[v, :, 0:128] = jnp.where(first_half, tail, head)
        high, low = split_two(state_ref[v])
        faces_ref[v, :, 128:384] = product(high, selection) + product(low, selection)


def faces_kernel(state_ref, select_ref, faces_ref):
    write_faces(state_ref, select_ref, faces_ref)


def step_kernel(
    mix_ref,
    speed_ref,
    flow_ref,
    state_ref,
    prev_ref,
    own_ref,
    next_ref,
    pick_ref,
    expand_ref,
    rate_ref,
    select_ref,
    place_ref,
    segment_ref,
    out_ref,
    extra_ref,
    ghost_ref,
    spread_ref,
    gx_ref,
    last,
):
    variables = state_ref.shape[0]
    first_half = iota((64, 128), 1) < 64
    for d in range(3):
        lanes = slice(128 * d, 128 * d + 128)
        for v in range(variables):
            own = own_ref[v, :, lanes]
            table = jnp.concatenate(
                [prev_ref[v, :, lanes], own, next_ref[v, :, lanes], pltpu.roll(own, 64, 1)], axis=0
            )
            both = product(pick_ref[d], jnp.concatenate(split_two(table), axis=1))
            high = jnp.where(first_half, both[0:64, 0:128], both[64:128, 0:128])
            low = jnp.where(first_half, both[0:64, 128:256], both[64:128, 128:256])
            if d == 0:
                gx_ref[v] = high + low
            else:
                ghost_ref[d - 1, pl.ds(64 * v, 64), 0:128] = high.astype(jnp.bfloat16)
                ghost_ref[d - 1, pl.ds(64 * v, 64), 128:256] = low.astype(jnp.bfloat16)
    for d in range(2):
        spread_ref[d] = product(ghost_ref[d], expand_ref[d])

    lane = iota((8, 128), 1)
    lower_half = lane < 64
    y_low, y_top = lane // 8 % 8 == 0, lane // 8 % 8 == 7
    z_low, z_top = lane % 8 == 0, lane % 8 == 7

    def rows_step(group, carry):
        start = pl.multiple_of(8 * group, 8)
        rows = pl.ds(start, 8)
        rate = rate_ref[rows, :]
        for chunk in range(4):
            lanes = slice(128 * chunk, 128 * chunk + 128)
            diffs, values, smooth = [[], [], []], [], []
            for v in range(variables):
                u = state_ref[v, rows, lanes]
                middle = pltpu.roll(u, 64, 1)
                if chunk > 0:
                    below = pltpu.roll(state_ref[v, rows, 128 * chunk - 128 : 128 * chunk], 64, 1)
                else:
                    below = gx_ref[v, rows, :]
                if chunk < 3:
                    above = pltpu.roll(state_ref[v, rows, 128 * chunk + 128 : 128 * chunk + 256], 64, 1)
                else:
                    above = gx_ref[v, rows, :]
                spread_rows = pl.ds(pl.multiple_of(64 * v + start, 8), 8)
                gy = spread_ref[0, spread_rows, lanes]
                gz = spread_ref[1, spread_rows, lanes]
                pairs = [
                    (jnp.where(lower_half, below, middle), jnp.where(lower_half, middle, above)),
                    (
                        jnp.where(y_low, gy, pltpu.roll(u, 8, 1)),
                        jnp.where(y_top, gy, pltpu.roll(u, 120, 1)),
                    ),
                    (
                        jnp.where(z_low, gz, pltpu.roll(u, 1, 1)),
                        jnp.where(z_top, gz, pltpu.roll(u, 127, 1)),
                    ),
                ]
                twice = u + u
                total = None
                for d in range(3):
                    lower, upper = pairs[d]
                    diffs[d].append(upper - lower)
                    term = speed_ref[d] * ((upper - twice) + lower)
                    total = term if total is None else total + term
                values.append(u)
                smooth.append(total)
            for i in range(variables):
                change = -smooth[i]
                for d in range(3):
                    for j in range(variables):
                        change = change + mix_ref[64 * d + 8 * i + j] * diffs[d][j]
                out_ref[i, rows, lanes] = values[i] - rate * change
        return carry

    lax.fori_loop(0, 8, rows_step, 0)
    if last:
        total = flow_ref[0] * out_ref[0]
        for v in range(1, variables):
            total = total + flow_ref[v] * out_ref[v]
        patches = sum_of_parts(product_of_parts(split_three(total), select_ref[...]))
        parts = jnp.concatenate(split_three(patches) + (segment_ref[...],), axis=1)
        sent = [product(place_ref[0], parts), product(place_ref[1], parts)]
        for k in range(2):
            extra_ref[:, 128 * k : 128 * k + 128] = sum_of_parts(
                [sent[k][:, 128 * i : 128 * i + 128] for i in range(3)]
            )
        extra_ref[:, 256:384] = jnp.where(
            iota((128, 128), 1) < 64, sent[0][:, 384:512], sent[1][:, 384:512]
        )
    else:
        write_faces(out_ref, select_ref, extra_ref)


SMEM_SPEC = pl.BlockSpec(memory_space=pltpu.SMEM)
VMEM_SPEC = pl.BlockSpec(memory_space=pltpu.VMEM)
INTERPRET = False


def on_chip(*values):
    if INTERPRET:
        return values
    return tuple(pltpu.with_memory_space_constraint(value, pltpu.VMEM) for value in values)


def make_faces(state_in, selection):
    return pl.pallas_call(
        faces_kernel,
        out_shape=jax.ShapeDtypeStruct(state_in.shape[:2] + (384,), jnp.float32),
        in_specs=[VMEM_SPEC] * 2,
        out_specs=VMEM_SPEC,
        interpret=INTERPRET,
    )(state_in, selection)


def advance(mix, speeds, flow, state_in, prev, own, following, pick, expand, rate, selection, place, segment, last):
    variables, blocks = state_in.shape[:2]
    extra = (128, 384) if last else (variables, blocks, 384)
    return pl.pallas_call(
        functools.partial(step_kernel, last=last),
        out_shape=(
            jax.ShapeDtypeStruct(state_in.shape, jnp.float32),
            jax.ShapeDtypeStruct(extra, jnp.float32),
        ),
        in_specs=[SMEM_SPEC] * 3 + [VMEM_SPEC] * 10,
        out_specs=(VMEM_SPEC, VMEM_SPEC),
        scratch_shapes=[
            pltpu.VMEM((2, 64 * variables, 256), jnp.bfloat16),
            pltpu.VMEM((2, 64 * variables, 512), jnp.float32),
            pltpu.VMEM((variables, 64, 128), jnp.float32),
        ],
        interpret=INTERPRET,
    )(
        mix,
        speeds,
        flow,
        state_in, *on_chip(prev, own, following, pick, expand, rate, selection), place, segment,
    )


def block_picks(neighbours, offset):
    blocks = neighbours.shape[0]
    local = jnp.where(
        neighbours >= 0, neighbours - offset, 3 * blocks + jnp.arange(blocks, dtype=jnp.int32)[:, None]
    )
    index = jnp.transpose(local).reshape(3, 2 * blocks)
    return (index[:, :, None] == iota((3, 2 * blocks, 4 * blocks), 2)).astype(jnp.bfloat16)


def wave_speeds(flux_derivative_matrices):
    return jnp.max(jnp.sum(jnp.abs(flux_derivative_matrices), axis=2), axis=1)


def transform_tables():
    column = np.arange(64)
    q, imaginary = 2 * (column // 8) + column % 2, column // 4 % 2 == 1
    s, r, n = np.arange(16), np.arange(64), np.arange(32)
    step = 2.0 * np.pi * np.outer(s, q) / 16
    twist = 2.0 * np.pi * np.outer(r, q) / NLON
    wave = 2.0 * np.pi * np.outer(n, r) / 64
    split = np.concatenate([np.cos(step), -np.sin(step)], axis=1)
    twiddle = np.stack([np.cos(twist), np.sin(twist)])
    forward = np.concatenate([np.cos(wave), np.sin(wave)], axis=1) / NLON
    backward = np.concatenate([np.cos(wave), np.sin(wave)], axis=0).T
    factor = np.where((n[:, None] == 0) & (q[None, :] == 0), 1.0, 2.0)
    untwist = np.stack(
        [
            np.where(imaginary, -np.sin(twist), np.cos(twist)),
            np.where(imaginary, -np.cos(twist), -np.sin(twist)),
        ]
    )
    of_latitude = [(column // 2 % 2 == latitude)[None, :] for latitude in range(2)]
    join = np.concatenate(
        [np.concatenate([np.cos(step) * own, np.sin(step) * own], axis=1) for own in of_latitude]
    )
    return [
        jnp.asarray(table.astype(np.float32))
        for table in (split, twiddle, forward, factor, backward, untwist, join)
    ]


def landing_of(codes, k):
    return codes[:, 64 * k : 64 * k + 16] == (iota((128, 16), 1) + 1).astype(jnp.float32)


def forward_kernel(got_ref, split_ref, twiddle_ref, forward_ref, grid_ref, send_ref):
    grid = None
    codes = got_ref[:, 256:384]
    for k in range(2):
        landing = landing_of(codes, k).astype(jnp.float32)
        part = exact(landing, got_ref[:, 128 * k : 128 * k + 128], 0, 0)
        grid = part if grid is None else grid + part
    grid_ref[...] = grid
    column = iota((64, 64), 1)
    split = split_ref[...]
    first, second = exact(grid[:, 0:64], split, 0, 0), exact(grid[:, 64:128], split, 0, 0)
    of_first = column // 2 % 2 == 0
    even = jnp.where(of_first, first[:, 0:64], second[:, 0:64])
    odd = jnp.where(of_first, first[:, 64:128], second[:, 64:128])
    turned_re = even * twiddle_ref[0] + odd * twiddle_ref[1]
    turned_im = odd * twiddle_ref[0] - even * twiddle_ref[1]
    real = column // 4 % 2 == 0
    both = jnp.concatenate(
        [jnp.where(real, turned_re, turned_im), jnp.where(real, turned_im, -turned_re)], axis=0
    )
    coef = exact(forward_ref[...], both)
    for part in range(8):
        send_ref[32 * part : 32 * part + 32, :] = coef[:, 8 * part : 8 * part + 8]


def backward_kernel(
    synth_ref, got_ref, factor_ref, backward_ref, untwist_ref, join_ref, grid_ref, back_ref, pair_ref
):
    for part in range(8):
        columns = slice(8 * part, 8 * part + 8)
        values = synth_ref[32 * part : 32 * part + 32, :]
        pair_ref[0:32, columns] = values
        pair_ref[32:64, columns] = jnp.concatenate([-values[:, 4:8], values[:, 0:4]], axis=1)
    factor = factor_ref[...]
    pair = pair_ref[...] * jnp.concatenate([factor, factor], axis=0)
    rows = exact(backward_ref[...], pair)
    turned = jnp.concatenate([rows * untwist_ref[0], rows * untwist_ref[1]], axis=1)
    joined = exact(join_ref[...], turned, 1, 1)
    grid_ref[:, 0:64] = joined[0:16]
    grid_ref[:, 64:128] = joined[16:32]
    parts = jnp.concatenate(split_three(grid_ref[...]), axis=1)
    codes = got_ref[:, 256:384]
    for k in range(2):
        found = product(landing_of(codes, k).astype(jnp.float32).astype(jnp.bfloat16), parts)
        back_ref[:, 128 * k : 128 * k + 128] = sum_of_parts(
            [found[:, 128 * i : 128 * i + 128] for i in range(3)]
        )


def home_kernel(home_ref, place_ref, shell_ref):
    total = None
    for k in range(2):
        parts = jnp.concatenate(split_three(home_ref[:, 128 * k : 128 * k + 128]), axis=1)
        found = lax.dot_general(
            place_ref[k], parts, (((0,), (0,)), ((), ())), preferred_element_type=jnp.float32
        )
        part = sum_of_parts([found[:, 128 * i : 128 * i + 128] for i in range(3)])
        total = part if total is None else total + part
    shell_ref[...] = total


def run_kernel(kernel, operands, shapes, scratch=()):
    return pl.pallas_call(
        kernel,
        out_shape=tuple(jax.ShapeDtypeStruct(shape, jnp.float32) for shape in shapes),
        in_specs=[VMEM_SPEC] * len(operands),
        out_specs=tuple([VMEM_SPEC] * len(shapes)),
        scratch_shapes=[pltpu.VMEM(shape, jnp.float32) for shape in scratch],
        interpret=INTERPRET,
    )(*on_chip(*operands))


def legendre_start(sine_lat, orders):
    series_k = jnp.arange(1, DEGREES, dtype=jnp.int32).astype(jnp.float32)
    log_sums = jnp.concatenate(
        [
            jnp.zeros((1,), jnp.float32),
            jnp.cumsum(0.5 * jnp.log((2.0 * series_k + 1.0) / (2.0 * series_k))),
        ]
    )
    log_base = jnp.take(log_sums, orders)
    return jnp.exp(0.5 * math.log(0.5) + log_base + orders.astype(jnp.float32) * jnp.log(sine_lat))


def recurrence_factors(orders):
    degree = iota((DEGREES, orders.shape[0]), 0)
    order = jnp.broadcast_to(orders[None, :], degree.shape)
    degree_real, order_real = degree.astype(jnp.float32), order.astype(jnp.float32)
    ratio_up = jnp.sqrt(
        jnp.maximum(4.0 * degree_real * degree_real - 1.0, 1.0)
        / jnp.maximum(degree_real * degree_real - order_real * order_real, 1.0)
    )
    lower_deg = degree_real - 1.0
    ratio_back = jnp.sqrt(
        jnp.maximum(lower_deg * lower_deg - order_real * order_real, 0.0)
        / jnp.maximum(4.0 * lower_deg * lower_deg - 1.0, 1.0)
    )
    coef_prev = jnp.where(
        degree == order + 1,
        jnp.sqrt(2.0 * order_real + 3.0),
        jnp.where(degree >= order + 2, ratio_up, 0.0),
    )
    coef_before = jnp.where(degree >= order + 2, -ratio_up * ratio_back, 0.0)
    return coef_prev, coef_before


def spectral_kernel(
    first_ref, prev_ref, before_ref, gain_ref, re_ref, im_ref, diagonal_ref, cosine_ref, out_re, out_im
):
    even = iota((8, 128), 0) % 2 == 0
    order = first_ref[0] + iota((8, 128), 0) % 2
    rows_re, rows_im = re_ref[...], im_ref[...]
    diagonal, cosine = diagonal_ref[...], cosine_ref[...]
    zero = jnp.zeros((8, 128), jnp.float32)

    def over_latitudes(value):
        value = value + pltpu.roll(value, 4, 0)
        value = value + pltpu.roll(value, 2, 0)
        return jnp.sum(value, axis=1, keepdims=True)

    def some_degrees(step, carried):
        previous, before, acc_re, acc_im = carried
        for inner in range(16):
            degree = 16 * step + inner
            up = jnp.where(even, prev_ref[2 * degree], prev_ref[2 * degree + 1])
            back = jnp.where(even, before_ref[2 * degree], before_ref[2 * degree + 1])
            present = (up * cosine) * previous + back * before
            present = jnp.where(order == degree, diagonal, present)
            gain = gain_ref[degree]
            acc_re = acc_re + (gain * over_latitudes(rows_re * present)) * present
            acc_im = acc_im + (gain * over_latitudes(rows_im * present)) * present
            previous, before = present, previous
        return previous, before, acc_re, acc_im

    carried = lax.fori_loop(0, DEGREES // 16, some_degrees, (zero, zero, zero, zero))
    out_re[...] = carried[2]
    out_im[...] = carried[3]


def solve_spectral(received, first_order, lat_total):
    rows = received.reshape(2, 128, 2, 4).transpose(2, 0, 3, 1).reshape(2, 8, 128)
    row, lane = iota((8, 128), 0), iota((8, 128), 1)
    lat_ids = 256 * (row // 4) + 2 * lane + row // 2 % 2
    colatitude = (lat_ids.astype(jnp.float32) + 0.5) * (math.pi / lat_total)
    cosine, sine = jnp.cos(colatitude), jnp.sin(colatitude)
    weights = math.pi / lat_total * sine
    orders = first_order + jnp.arange(2, dtype=jnp.int32)
    diagonal = legendre_start(sine, jnp.broadcast_to(jnp.tile(orders, 4)[:, None], (8, 128)))
    coef_prev, coef_before = recurrence_factors(orders)
    degree_real = jnp.arange(DEGREES, dtype=jnp.int32).astype(jnp.float32)
    gain = POT_GAIN / (degree_real * (degree_real + 1.0) + KAPPA2)
    shape = jax.ShapeDtypeStruct((8, 128), jnp.float32)
    acc_re, acc_im = pl.pallas_call(
        spectral_kernel,
        out_shape=(shape, shape),
        in_specs=[SMEM_SPEC] * 4 + [VMEM_SPEC] * 4,
        out_specs=(VMEM_SPEC, VMEM_SPEC),
        interpret=INTERPRET,
    )(
        orders[0:1],
        coef_prev.reshape(-1),
        coef_before.reshape(-1),
        gain,
        *on_chip(rows[0] * weights, rows[1] * weights, diagonal, cosine),
    )
    both = jnp.stack([acc_re, acc_im]).reshape(2, 2, 4, 128)
    return both.transpose(1, 3, 0, 2).reshape(256, 8)


def body(
    invariant_fluid_quantities,
    flux_derivative_matrices,
    levels,
    neighbours,
    block_latitude_band,
    block_longitude_segment,
    parallel_flow_coefficients,
):
    grp_size = lax.axis_size("grp")
    core_size = lax.axis_size("cores")
    device_total = grp_size * core_size
    block_portion = invariant_fluid_quantities.shape[1]
    state_variables = invariant_fluid_quantities.shape[0]
    device = lax.axis_index(("grp", "cores"))
    speeds = wave_speeds(flux_derivative_matrices)
    rate_block = COURANT * jnp.exp2(levels.astype(jnp.float32) - (LEVELS - 1)) / jnp.max(speeds)
    offset = (device - 1) * block_portion
    picks = block_picks(neighbours, offset)
    selection, expand = face_selection(), ghost_expansion()
    rate = jnp.broadcast_to(rate_block[:, None], (block_portion, 128))
    mix = 0.5 * flux_derivative_matrices.reshape(-1)
    half_speeds = 0.5 * speeds
    band_index = block_latitude_band[:, 0]
    block_ids = jnp.arange(block_portion, dtype=jnp.int32)
    earlier = (band_index[None, :] == band_index[:, None]) & (
        block_ids[None, :] < block_ids[:, None]
    )
    rank_in_band = jnp.sum(earlier.astype(jnp.int32), axis=1)
    shape = (2, grp_size, block_portion)
    place = (
        (band_index[None, None, :] == iota(shape, 1)) & (rank_in_band[None, None, :] == iota(shape, 0))
    ).astype(jnp.bfloat16)
    segment = jnp.broadcast_to(
        (block_longitude_segment + 1).astype(jnp.bfloat16)[:, None], (block_portion, 128)
    )
    parallel_flow_charge = invariant_fluid_quantities
    faces = make_faces(parallel_flow_charge, selection)
    for section_index in range(STEPS):
        last = section_index == STEPS - 1
        parallel_flow_charge, faces = advance(
            mix,
            half_speeds,
            parallel_flow_coefficients,
            parallel_flow_charge,
            passed_along(faces, ("grp", "cores"), 1),
            faces,
            passed_along(faces, ("grp", "cores"), -1),
            picks,
            expand,
            rate,
            patch_selection() if last else selection,
            place,
            segment,
            last,
        )
    split, twiddle, forward, factor, backward, untwist, join = transform_tables()
    got = lax.all_to_all(faces, "grp", split_axis=0, concat_axis=0, tiled=True)
    fac_segments, coef = run_kernel(
        forward_kernel, (got, split, twiddle, forward), ((16, 128), (device_total, 8))
    )
    axes = ("grp", "cores")
    received = lax.all_to_all(coef, axes, split_axis=0, concat_axis=0, tiled=True)
    synth = solve_spectral(received, 16 * (device % 32) + 2 * (device // 32), LAT_DEV * device_total)
    returned = lax.all_to_all(synth, axes, split_axis=0, concat_axis=0, tiled=True)
    grid_segments, back = run_kernel(
        backward_kernel,
        (returned, got, factor, backward, untwist, join),
        ((16, 128), (grp_size, 256)),
        scratch=((64, 64),),
    )
    home = lax.all_to_all(back, "grp", split_axis=0, concat_axis=0, tiled=True)
    (shell_potential,) = run_kernel(home_kernel, (home, place), ((block_portion, 128),))
    fac_local, potential_local = (
        jnp.swapaxes(grid.reshape(16, LAT_DEV, 64), 0, 1).reshape(LAT_DEV, NLON)
        for grid in (fac_segments, grid_segments)
    )
    return (parallel_flow_charge, fac_local, potential_local, shell_potential)


def solution(mesh):
    placed = (
        P(None, ("grp", "cores"), None),
        P(),
        P(("grp", "cores")),
        P(("grp", "cores"), None),
        P(("grp", "cores"), None),
        P(("grp", "cores")),
        P(),
    )
    return jax.shard_map(
        body,
        mesh=mesh,
        in_specs=placed,
        out_specs=(
            P(None, ("grp", "cores"), None),
            P(("grp", "cores"), None),
            P(("grp", "cores"), None),
            P(("grp", "cores"), None),
        ),
        check_vma=False,
    )
```

```python
import functools
import math

import jax
import jax.numpy as jnp
import numpy as np
from jax import lax
from jax.experimental import pallas as pl
from jax.experimental.pallas import tpu as pltpu
from jax.sharding import PartitionSpec as P

LEVELS = 4
STEPS = 2
LAT_DEV = 2
NLON = 1024
DEGREES = 512


COURANT = 0.3
KAPPA2 = 400.0
POT_GAIN = 2000.0
HIGHEST_PRECISION = lax.Precision.HIGHEST


def passed_along(value, axis, steps):
    count = lax.axis_size(axis)
    leading, last = (max(0, -steps), min(count, count - steps))
    return lax.ppermute(value, axis, [(source, source + steps) for source in range(leading, last)])


def iota(shape, dim):
    return lax.broadcasted_iota(jnp.int32, shape, dim)


def face_selection():
    cell, col = iota((512, 256), 0), iota((512, 256), 1)
    face, c = col // 64, col % 64
    along_y = 64 * (c // 8) + jnp.where(face == 0, 56, 0) + c % 8
    along_z = 64 * (c // 8) + 8 * (c % 8) + jnp.where(face == 2, 7, 0)
    return (cell == jnp.where(face < 2, along_y, along_z)).astype(jnp.bfloat16)


def ghost_expansion():
    shape = (2, 256, 512)
    along, row, cell = iota(shape, 0), iota(shape, 1) % 128, iota(shape, 2)
    c, top = row % 64, row // 64
    target_y = 64 * (c // 8) + 56 * top + c % 8
    target_z = 64 * (c // 8) + 8 * (c % 8) + 7 * top
    return (cell == jnp.where(along == 0, target_y, target_z)).astype(jnp.bfloat16)


def patch_selection():
    cell, k = iota((512, 128), 0), iota((512, 128), 1)
    return (cell == 8 * (k % 64) + k // 64).astype(jnp.bfloat16)


def split_two(value):
    high = value.astype(jnp.bfloat16)
    return high, (value - high.astype(jnp.float32)).astype(jnp.bfloat16)


def split_three(value):
    high = value.astype(jnp.bfloat16)
    return (high,) + split_two(value - high.astype(jnp.float32))


def sum_of_parts(parts):
    return parts[0] + (parts[1] + parts[2])


def product_of_parts(parts, right):
    return [product(part, right) for part in parts]


def exact(left, right, left_dim=1, right_dim=0):
    return lax.dot_general(
        left,
        right,
        (((left_dim,), (right_dim,)), ((), ())),
        precision=HIGHEST_PRECISION,
        preferred_element_type=jnp.float32,
    )


def product(left, right):
    return jnp.dot(left, right, preferred_element_type=jnp.float32)


def write_faces(state_ref, select_ref, faces_ref):
    first_half = iota((64, 128), 1) < 64
    selection = select_ref[...]
    for v in range(state_ref.shape[0]):
        head = pltpu.roll(state_ref[v, :, 0:128], 64, 1)
        tail = pltpu.roll(state_ref[v, :, 384:512], 64, 1)
        faces_ref[v, :, 0:128] = jnp.where(first_half, tail, head)
        high, low = split_two(state_ref[v])
        faces_ref[v, :, 128:384] = product(high, selection) + product(low, selection)


def faces_kernel(state_ref, select_ref, faces_ref):
    write_faces(state_ref, select_ref, faces_ref)


def step_kernel(
    mix_ref,
    speed_ref,
    flow_ref,
    state_ref,
    prev_ref,
    own_ref,
    next_ref,
    pick_ref,
    expand_ref,
    rate_ref,
    select_ref,
    place_ref,
    segment_ref,
    out_ref,
    extra_ref,
    ghost_ref,
    spread_ref,
    gx_ref,
    last,
):
    variables = state_ref.shape[0]
    first_half = iota((64, 128), 1) < 64
    for d in range(3):
        lanes = slice(128 * d, 128 * d + 128)
        for v in range(variables):
            own = own_ref[v, :, lanes]
            table = jnp.concatenate(
                [prev_ref[v, :, lanes], own, next_ref[v, :, lanes], pltpu.roll(own, 64, 1)], axis=0
            )
            both = product(pick_ref[d], jnp.concatenate(split_two(table), axis=1))
            high = jnp.where(first_half, both[0:64, 0:128], both[64:128, 0:128])
            low = jnp.where(first_half, both[0:64, 128:256], both[64:128, 128:256])
            if d == 0:
                gx_ref[v] = high + low
            else:
                ghost_ref[d - 1, pl.ds(64 * v, 64), 0:128] = high.astype(jnp.bfloat16)
                ghost_ref[d - 1, pl.ds(64 * v, 64), 128:256] = low.astype(jnp.bfloat16)
    for d in range(2):
        spread_ref[d] = product(ghost_ref[d], expand_ref[d])

    lane = iota((8, 128), 1)
    lower_half = lane < 64
    y_low, y_top = lane // 8 % 8 == 0, lane // 8 % 8 == 7
    z_low, z_top = lane % 8 == 0, lane % 8 == 7

    def rows_step(group, carry):
        start = pl.multiple_of(8 * group, 8)
        rows = pl.ds(start, 8)
        rate = rate_ref[rows, :]
        for chunk in range(4):
            lanes = slice(128 * chunk, 128 * chunk + 128)
            diffs, values, smooth = [[], [], []], [], []
            for v in range(variables):
                u = state_ref[v, rows, lanes]
                middle = pltpu.roll(u, 64, 1)
                if chunk > 0:
                    below = pltpu.roll(state_ref[v, rows, 128 * chunk - 128 : 128 * chunk], 64, 1)
                else:
                    below = gx_ref[v, rows, :]
                if chunk < 3:
                    above = pltpu.roll(state_ref[v, rows, 128 * chunk + 128 : 128 * chunk + 256], 64, 1)
                else:
                    above = gx_ref[v, rows, :]
                spread_rows = pl.ds(pl.multiple_of(64 * v + start, 8), 8)
                gy = spread_ref[0, spread_rows, lanes]
                gz = spread_ref[1, spread_rows, lanes]
                pairs = [
                    (jnp.where(lower_half, below, middle), jnp.where(lower_half, middle, above)),
                    (
                        jnp.where(y_low, gy, pltpu.roll(u, 8, 1)),
                        jnp.where(y_top, gy, pltpu.roll(u, 120, 1)),
                    ),
                    (
                        jnp.where(z_low, gz, pltpu.roll(u, 1, 1)),
                        jnp.where(z_top, gz, pltpu.roll(u, 127, 1)),
                    ),
                ]
                twice = u + u
                total = None
                for d in range(3):
                    lower, upper = pairs[d]
                    diffs[d].append(upper - lower)
                    term = speed_ref[d] * ((upper - twice) + lower)
                    total = term if total is None else total + term
                values.append(u)
                smooth.append(total)
            for i in range(variables):
                change = -smooth[i]
                for d in range(3):
                    for j in range(variables):
                        change = change + mix_ref[64 * d + 8 * i + j] * diffs[d][j]
                out_ref[i, rows, lanes] = values[i] - rate * change
        return carry

    lax.fori_loop(0, 8, rows_step, 0)
    if last:
        total = flow_ref[0] * out_ref[0]
        for v in range(1, variables):
            total = total + flow_ref[v] * out_ref[v]
        patches = sum_of_parts(product_of_parts(split_three(total), select_ref[...]))
        parts = jnp.concatenate(split_three(patches) + (segment_ref[...],), axis=1)
        sent = [product(place_ref[0], parts), product(place_ref[1], parts)]
        for k in range(2):
            extra_ref[:, 0, 128 * k : 128 * k + 128] = sum_of_parts(
                [sent[k][:, 128 * i : 128 * i + 128] for i in range(3)]
            )
        extra_ref[:, 0, 256:384] = jnp.where(
            iota((128, 128), 1) < 64, sent[0][:, 384:512], sent[1][:, 384:512]
        )
    else:
        write_faces(out_ref, select_ref, extra_ref)


SMEM_SPEC = pl.BlockSpec(memory_space=pltpu.SMEM)
VMEM_SPEC = pl.BlockSpec(memory_space=pltpu.VMEM)
INTERPRET = False


def on_chip(*values):
    if INTERPRET:
        return values
    return tuple(pltpu.with_memory_space_constraint(value, pltpu.VMEM) for value in values)


def make_faces(state_in, selection):
    return pl.pallas_call(
        faces_kernel,
        out_shape=jax.ShapeDtypeStruct(state_in.shape[:2] + (384,), jnp.float32),
        in_specs=[VMEM_SPEC] * 2,
        out_specs=VMEM_SPEC,
        interpret=INTERPRET,
    )(state_in, selection)


def advance(mix, speeds, flow, state_in, prev, own, following, pick, expand, rate, selection, place, segment, last):
    variables, blocks = state_in.shape[:2]
    (prev, following), shared = on_chip(prev, following), (pick, expand, rate, selection)
    if not last:
        own, *shared = on_chip(own, *shared)
    operands = (state_in, prev, own, following, *shared, place, segment)
    extra = (128, 1, 384) if last else (variables, blocks, 384)
    return pl.pallas_call(
        functools.partial(step_kernel, last=last),
        out_shape=(
            jax.ShapeDtypeStruct(state_in.shape, jnp.float32),
            jax.ShapeDtypeStruct(extra, jnp.float32),
        ),
        in_specs=[SMEM_SPEC] * 3 + [VMEM_SPEC] * 10,
        out_specs=(VMEM_SPEC, VMEM_SPEC),
        scratch_shapes=[
            pltpu.VMEM((2, 64 * variables, 256), jnp.bfloat16),
            pltpu.VMEM((2, 64 * variables, 512), jnp.float32),
            pltpu.VMEM((variables, 64, 128), jnp.float32),
        ],
        interpret=INTERPRET,
    )(
        mix,
        speeds,
        flow,
        *operands,
    )


def block_picks(neighbours, offset):
    blocks = neighbours.shape[0]
    local = jnp.where(
        neighbours >= 0, neighbours - offset, 3 * blocks + jnp.arange(blocks, dtype=jnp.int32)[:, None]
    )
    index = jnp.transpose(local).reshape(3, 2 * blocks)
    return (index[:, :, None] == iota((3, 2 * blocks, 4 * blocks), 2)).astype(jnp.bfloat16)


def wave_speeds(flux_derivative_matrices):
    return jnp.max(jnp.sum(jnp.abs(flux_derivative_matrices), axis=2), axis=1)


def transform_tables():
    column = np.arange(64)
    q, imaginary = 2 * (column // 8) + column % 2, column // 4 % 2 == 1
    s, r, n = np.arange(16), np.arange(64), np.arange(32)
    step = 2.0 * np.pi * np.outer(s, q) / 16
    twist = 2.0 * np.pi * np.outer(r, q) / NLON
    wave = 2.0 * np.pi * np.outer(n, r) / 64
    split = np.concatenate([np.cos(step), -np.sin(step)], axis=1)
    twiddle = np.stack([np.cos(twist), np.sin(twist)])
    forward = np.concatenate([np.cos(wave), np.sin(wave)], axis=1) / NLON
    backward = np.concatenate([np.cos(wave), np.sin(wave)], axis=0).T
    factor = np.where((n[:, None] == 0) & (q[None, :] == 0), 1.0, 2.0)
    untwist = np.stack(
        [
            np.where(imaginary, -np.sin(twist), np.cos(twist)),
            np.where(imaginary, -np.cos(twist), -np.sin(twist)),
        ]
    )
    of_latitude = [(column // 2 % 2 == latitude)[None, :] for latitude in range(2)]
    join = np.concatenate(
        [np.concatenate([np.cos(step) * own, np.sin(step) * own], axis=1) for own in of_latitude]
    )
    return [
        jnp.asarray(table.astype(np.float32))
        for table in (split, twiddle, forward, factor, backward, untwist, join)
    ]


def landing_of(codes, k):
    return codes[:, 64 * k : 64 * k + 16] == (iota((128, 16), 1) + 1).astype(jnp.float32)


def forward_kernel(got_ref, split_ref, twiddle_ref, forward_ref, grid_ref, send_ref):
    grid = None
    codes = got_ref[:, 256:384]
    for k in range(2):
        landing = landing_of(codes, k).astype(jnp.float32)
        part = exact(landing, got_ref[:, 128 * k : 128 * k + 128], 0, 0)
        grid = part if grid is None else grid + part
    grid_ref[...] = grid
    column = iota((64, 64), 1)
    split = split_ref[...]
    first, second = exact(grid[:, 0:64], split, 0, 0), exact(grid[:, 64:128], split, 0, 0)
    of_first = column // 2 % 2 == 0
    even = jnp.where(of_first, first[:, 0:64], second[:, 0:64])
    odd = jnp.where(of_first, first[:, 64:128], second[:, 64:128])
    turned_re = even * twiddle_ref[0] + odd * twiddle_ref[1]
    turned_im = odd * twiddle_ref[0] - even * twiddle_ref[1]
    real = column // 4 % 2 == 0
    both = jnp.concatenate(
        [jnp.where(real, turned_re, turned_im), jnp.where(real, turned_im, -turned_re)], axis=0
    )
    coef = exact(forward_ref[...], both)
    for part in range(8):
        send_ref[32 * part : 32 * part + 32, :] = coef[:, 8 * part : 8 * part + 8]


def backward_kernel(
    synth_ref, got_ref, factor_ref, backward_ref, untwist_ref, join_ref, grid_ref, back_ref, pair_ref
):
    for part in range(8):
        columns = slice(8 * part, 8 * part + 8)
        values = synth_ref[32 * part : 32 * part + 32, :]
        pair_ref[0:32, columns] = values
        pair_ref[32:64, columns] = jnp.concatenate([-values[:, 4:8], values[:, 0:4]], axis=1)
    factor = factor_ref[...]
    pair = pair_ref[...] * jnp.concatenate([factor, factor], axis=0)
    rows = exact(backward_ref[...], pair)
    turned = jnp.concatenate([rows * untwist_ref[0], rows * untwist_ref[1]], axis=1)
    joined = exact(join_ref[...], turned, 1, 1)
    grid_ref[:, 0:64] = joined[0:16]
    grid_ref[:, 64:128] = joined[16:32]
    parts = jnp.concatenate(split_three(grid_ref[...]), axis=1)
    codes = got_ref[:, 256:384]
    for k in range(2):
        found = product(landing_of(codes, k).astype(jnp.float32).astype(jnp.bfloat16), parts)
        back_ref[:, 0, 128 * k : 128 * k + 128] = sum_of_parts(
            [found[:, 128 * i : 128 * i + 128] for i in range(3)]
        )


def home_kernel(home_ref, place_ref, shell_ref):
    total = None
    for k in range(2):
        parts = jnp.concatenate(split_three(home_ref[:, 128 * k : 128 * k + 128]), axis=1)
        found = lax.dot_general(
            place_ref[k], parts, (((0,), (0,)), ((), ())), preferred_element_type=jnp.float32
        )
        part = sum_of_parts([found[:, 128 * i : 128 * i + 128] for i in range(3)])
        total = part if total is None else total + part
    shell_ref[...] = total


def run_kernel(kernel, operands, shapes, scratch=()):
    return pl.pallas_call(
        kernel,
        out_shape=tuple(jax.ShapeDtypeStruct(shape, jnp.float32) for shape in shapes),
        in_specs=[VMEM_SPEC] * len(operands),
        out_specs=tuple([VMEM_SPEC] * len(shapes)),
        scratch_shapes=[pltpu.VMEM(shape, jnp.float32) for shape in scratch],
        interpret=INTERPRET,
    )(*on_chip(*operands))


def legendre_start(sine_lat, orders):
    series_k = jnp.arange(1, DEGREES, dtype=jnp.int32).astype(jnp.float32)
    log_sums = jnp.concatenate(
        [
            jnp.zeros((1,), jnp.float32),
            jnp.cumsum(0.5 * jnp.log((2.0 * series_k + 1.0) / (2.0 * series_k))),
        ]
    )
    log_base = jnp.take(log_sums, orders)
    return jnp.exp(0.5 * math.log(0.5) + log_base + orders.astype(jnp.float32) * jnp.log(sine_lat))


def recurrence_factors(orders):
    degree = iota((DEGREES, orders.shape[0]), 0)
    order = jnp.broadcast_to(orders[None, :], degree.shape)
    degree_real, order_real = degree.astype(jnp.float32), order.astype(jnp.float32)
    ratio_up = jnp.sqrt(
        jnp.maximum(4.0 * degree_real * degree_real - 1.0, 1.0)
        / jnp.maximum(degree_real * degree_real - order_real * order_real, 1.0)
    )
    lower_deg = degree_real - 1.0
    ratio_back = jnp.sqrt(
        jnp.maximum(lower_deg * lower_deg - order_real * order_real, 0.0)
        / jnp.maximum(4.0 * lower_deg * lower_deg - 1.0, 1.0)
    )
    coef_prev = jnp.where(
        degree == order + 1,
        jnp.sqrt(2.0 * order_real + 3.0),
        jnp.where(degree >= order + 2, ratio_up, 0.0),
    )
    coef_before = jnp.where(degree >= order + 2, -ratio_up * ratio_back, 0.0)
    return coef_prev, coef_before


def spectral_kernel(
    first_ref, prev_ref, before_ref, gain_ref, re_ref, im_ref, diagonal_ref, cosine_ref, out_re, out_im
):
    even = iota((8, 128), 0) % 2 == 0
    order = first_ref[0] + iota((8, 128), 0) % 2
    rows_re, rows_im = re_ref[...], im_ref[...]
    diagonal, cosine = diagonal_ref[...], cosine_ref[...]
    zero = jnp.zeros((8, 128), jnp.float32)

    def over_latitudes(value):
        value = value + pltpu.roll(value, 4, 0)
        value = value + pltpu.roll(value, 2, 0)
        return jnp.sum(value, axis=1, keepdims=True)

    def some_degrees(step, carried):
        previous, before, acc_re, acc_im = carried
        for inner in range(16):
            degree = 16 * step + inner
            up = jnp.where(even, prev_ref[2 * degree], prev_ref[2 * degree + 1])
            back = jnp.where(even, before_ref[2 * degree], before_ref[2 * degree + 1])
            present = (up * cosine) * previous + back * before
            present = jnp.where(order == degree, diagonal, present)
            gain = gain_ref[degree]
            acc_re = acc_re + (gain * over_latitudes(rows_re * present)) * present
            acc_im = acc_im + (gain * over_latitudes(rows_im * present)) * present
            previous, before = present, previous
        return previous, before, acc_re, acc_im

    carried = lax.fori_loop(0, DEGREES // 16, some_degrees, (zero, zero, zero, zero))
    out_re[...] = carried[2]
    out_im[...] = carried[3]


def solve_spectral(received, first_order, lat_total):
    rows = received.reshape(2, 128, 2, 4).transpose(2, 0, 3, 1).reshape(2, 8, 128)
    row, lane = iota((8, 128), 0), iota((8, 128), 1)
    lat_ids = 256 * (row // 4) + 2 * lane + row // 2 % 2
    colatitude = (lat_ids.astype(jnp.float32) + 0.5) * (math.pi / lat_total)
    cosine, sine = jnp.cos(colatitude), jnp.sin(colatitude)
    weights = math.pi / lat_total * sine
    orders = first_order + jnp.arange(2, dtype=jnp.int32)
    diagonal = legendre_start(sine, jnp.broadcast_to(jnp.tile(orders, 4)[:, None], (8, 128)))
    coef_prev, coef_before = recurrence_factors(orders)
    degree_real = jnp.arange(DEGREES, dtype=jnp.int32).astype(jnp.float32)
    gain = POT_GAIN / (degree_real * (degree_real + 1.0) + KAPPA2)
    shape = jax.ShapeDtypeStruct((8, 128), jnp.float32)
    acc_re, acc_im = pl.pallas_call(
        spectral_kernel,
        out_shape=(shape, shape),
        in_specs=[SMEM_SPEC] * 4 + [VMEM_SPEC] * 4,
        out_specs=(VMEM_SPEC, VMEM_SPEC),
        interpret=INTERPRET,
    )(
        orders[0:1],
        coef_prev.reshape(-1),
        coef_before.reshape(-1),
        gain,
        *on_chip(rows[0] * weights, rows[1] * weights, diagonal, cosine),
    )
    both = jnp.stack([acc_re, acc_im]).reshape(2, 2, 4, 128)
    return both.transpose(1, 3, 0, 2).reshape(256, 8)


def body(
    invariant_fluid_quantities,
    flux_derivative_matrices,
    levels,
    neighbours,
    block_latitude_band,
    block_longitude_segment,
    parallel_flow_coefficients,
):
    grp_size = lax.axis_size("grp")
    core_size = lax.axis_size("cores")
    device_total = grp_size * core_size
    block_portion = invariant_fluid_quantities.shape[1]
    state_variables = invariant_fluid_quantities.shape[0]
    device = lax.axis_index(("grp", "cores"))
    speeds = wave_speeds(flux_derivative_matrices)
    rate_block = COURANT * jnp.exp2(levels.astype(jnp.float32) - (LEVELS - 1)) / jnp.max(speeds)
    offset = (device - 1) * block_portion
    picks = block_picks(neighbours, offset)
    selection, expand = face_selection(), ghost_expansion()
    rate = jnp.broadcast_to(rate_block[:, None], (block_portion, 128))
    mix = 0.5 * flux_derivative_matrices.reshape(-1)
    half_speeds = 0.5 * speeds
    band_index = block_latitude_band[:, 0]
    block_ids = jnp.arange(block_portion, dtype=jnp.int32)
    earlier = (band_index[None, :] == band_index[:, None]) & (
        block_ids[None, :] < block_ids[:, None]
    )
    rank_in_band = jnp.sum(earlier.astype(jnp.int32), axis=1)
    shape = (2, grp_size, block_portion)
    place = (
        (band_index[None, None, :] == iota(shape, 1)) & (rank_in_band[None, None, :] == iota(shape, 0))
    ).astype(jnp.bfloat16)
    segment = jnp.broadcast_to(
        (block_longitude_segment + 1).astype(jnp.bfloat16)[:, None], (block_portion, 128)
    )
    parallel_flow_charge = invariant_fluid_quantities
    faces = make_faces(parallel_flow_charge, selection)
    for section_index in range(STEPS):
        last = section_index == STEPS - 1
        parallel_flow_charge, faces = advance(
            mix,
            half_speeds,
            parallel_flow_coefficients,
            parallel_flow_charge,
            passed_along(faces, ("grp", "cores"), 1),
            faces,
            passed_along(faces, ("grp", "cores"), -1),
            picks,
            expand,
            rate,
            patch_selection() if last else selection,
            place,
            segment,
            last,
        )
    split, twiddle, forward, factor, backward, untwist, join = transform_tables()
    got = lax.all_to_all(faces, "grp", split_axis=0, concat_axis=0, tiled=True)
    got = got.reshape(grp_size, 384)
    fac_segments, coef = run_kernel(
        forward_kernel, (got, split, twiddle, forward), ((16, 128), (device_total, 8))
    )
    axes = ("grp", "cores")
    received = lax.all_to_all(coef, axes, split_axis=0, concat_axis=0, tiled=True)
    synth = solve_spectral(received, 16 * (device % 32) + 2 * (device // 32), LAT_DEV * device_total)
    returned = lax.all_to_all(synth, axes, split_axis=0, concat_axis=0, tiled=True)
    grid_segments, back = run_kernel(
        backward_kernel,
        (returned, got, factor, backward, untwist, join),
        ((16, 128), (grp_size, 1, 256)),
        scratch=((64, 64),),
    )
    home = lax.all_to_all(back, "grp", split_axis=0, concat_axis=0, tiled=True)
    home = home.reshape(grp_size, 256)
    (shell_potential,) = run_kernel(home_kernel, (home, place), ((block_portion, 128),))
    fac_local, potential_local = (
        jnp.swapaxes(grid.reshape(16, LAT_DEV, 64), 0, 1).reshape(LAT_DEV, NLON)
        for grid in (fac_segments, grid_segments)
    )
    return (parallel_flow_charge, fac_local, potential_local, shell_potential)


def solution(mesh):
    placed = (
        P(None, ("grp", "cores"), None),
        P(),
        P(("grp", "cores")),
        P(("grp", "cores"), None),
        P(("grp", "cores"), None),
        P(("grp", "cores")),
        P(),
    )
    return jax.shard_map(
        body,
        mesh=mesh,
        in_specs=placed,
        out_specs=(
            P(None, ("grp", "cores"), None),
            P(("grp", "cores"), None),
            P(("grp", "cores"), None),
            P(("grp", "cores"), None),
        ),
        check_vma=False,
    )
```

```python
import functools
import math

import jax
import jax.numpy as jnp
import numpy as np
from jax import lax
from jax.experimental import pallas as pl
from jax.experimental.pallas import tpu as pltpu
from jax.sharding import PartitionSpec as P

LEVELS = 4
STEPS = 2
LAT_DEV = 2
NLON = 1024
DEGREES = 512


COURANT = 0.3
KAPPA2 = 400.0
POT_GAIN = 2000.0
HIGHEST_PRECISION = lax.Precision.HIGHEST


def passed_along(value, axis, steps):
    count = lax.axis_size(axis)
    leading, last = (max(0, -steps), min(count, count - steps))
    return lax.ppermute(value, axis, [(source, source + steps) for source in range(leading, last)])


def iota(shape, dim):
    return lax.broadcasted_iota(jnp.int32, shape, dim)


def face_selection():
    cell, col = iota((512, 256), 0), iota((512, 256), 1)
    face, c = col // 64, col % 64
    along_y = 64 * (c // 8) + jnp.where(face == 0, 56, 0) + c % 8
    along_z = 64 * (c // 8) + 8 * (c % 8) + jnp.where(face == 2, 7, 0)
    return (cell == jnp.where(face < 2, along_y, along_z)).astype(jnp.bfloat16)


def ghost_expansion():
    shape = (2, 256, 512)
    along, row, cell = iota(shape, 0), iota(shape, 1) % 128, iota(shape, 2)
    c, top = row % 64, row // 64
    target_y = 64 * (c // 8) + 56 * top + c % 8
    target_z = 64 * (c // 8) + 8 * (c % 8) + 7 * top
    return (cell == jnp.where(along == 0, target_y, target_z)).astype(jnp.bfloat16)


def patch_selection():
    cell, k = iota((512, 128), 0), iota((512, 128), 1)
    return (cell == 8 * (k % 64) + k // 64).astype(jnp.bfloat16)


def split_two(value):
    high = value.astype(jnp.bfloat16)
    return high, (value - high.astype(jnp.float32)).astype(jnp.bfloat16)


def split_three(value):
    high = value.astype(jnp.bfloat16)
    return (high,) + split_two(value - high.astype(jnp.float32))


def sum_of_parts(parts):
    return parts[0] + (parts[1] + parts[2])


def product_of_parts(parts, right):
    return [product(part, right) for part in parts]


def exact(left, right, left_dim=1, right_dim=0):
    return lax.dot_general(
        left,
        right,
        (((left_dim,), (right_dim,)), ((), ())),
        precision=HIGHEST_PRECISION,
        preferred_element_type=jnp.float32,
    )


def product(left, right):
    return jnp.dot(left, right, preferred_element_type=jnp.float32)


def write_faces(state_ref, select_ref, faces_ref):
    first_half = iota((64, 128), 1) < 64
    selection = select_ref[...]
    for v in range(state_ref.shape[0]):
        head = pltpu.roll(state_ref[v, :, 0:128], 64, 1)
        tail = pltpu.roll(state_ref[v, :, 384:512], 64, 1)
        faces_ref[v, :, 0:128] = jnp.where(first_half, tail, head)
        high, low = split_two(state_ref[v])
        faces_ref[v, :, 128:384] = product(high, selection) + product(low, selection)


def faces_kernel(state_ref, select_ref, faces_ref):
    write_faces(state_ref, select_ref, faces_ref)


def step_kernel(
    mix_ref,
    speed_ref,
    flow_ref,
    state_ref,
    prev_ref,
    own_ref,
    next_ref,
    pick_ref,
    expand_ref,
    rate_ref,
    select_ref,
    place_ref,
    segment_ref,
    out_ref,
    extra_ref,
    ghost_ref,
    spread_ref,
    gx_ref,
    last,
):
    variables = state_ref.shape[0]
    first_half = iota((64, 128), 1) < 64
    for d in range(3):
        lanes = slice(128 * d, 128 * d + 128)
        for v in range(variables):
            own = own_ref[v, :, lanes]
            table = jnp.concatenate(
                [prev_ref[v, :, lanes], own, next_ref[v, :, lanes], pltpu.roll(own, 64, 1)], axis=0
            )
            both = product(pick_ref[d], jnp.concatenate(split_two(table), axis=1))
            high = jnp.where(first_half, both[0:64, 0:128], both[64:128, 0:128])
            low = jnp.where(first_half, both[0:64, 128:256], both[64:128, 128:256])
            if d == 0:
                gx_ref[v] = high + low
            else:
                ghost_ref[d - 1, pl.ds(64 * v, 64), 0:128] = high.astype(jnp.bfloat16)
                ghost_ref[d - 1, pl.ds(64 * v, 64), 128:256] = low.astype(jnp.bfloat16)
    for d in range(2):
        spread_ref[d] = product(ghost_ref[d], expand_ref[d])

    lane = iota((8, 128), 1)
    lower_half = lane < 64
    y_low, y_top = lane // 8 % 8 == 0, lane // 8 % 8 == 7
    z_low, z_top = lane % 8 == 0, lane % 8 == 7

    def rows_step(group, carry):
        start = pl.multiple_of(8 * group, 8)
        rows = pl.ds(start, 8)
        rate = rate_ref[rows, :]
        for chunk in range(4):
            lanes = slice(128 * chunk, 128 * chunk + 128)
            diffs, values, smooth = [[], [], []], [], []
            for v in range(variables):
                u = state_ref[v, rows, lanes]
                middle = pltpu.roll(u, 64, 1)
                if chunk > 0:
                    below = pltpu.roll(state_ref[v, rows, 128 * chunk - 128 : 128 * chunk], 64, 1)
                else:
                    below = gx_ref[v, rows, :]
                if chunk < 3:
                    above = pltpu.roll(state_ref[v, rows, 128 * chunk + 128 : 128 * chunk + 256], 64, 1)
                else:
                    above = gx_ref[v, rows, :]
                spread_rows = pl.ds(pl.multiple_of(64 * v + start, 8), 8)
                gy = spread_ref[0, spread_rows, lanes]
                gz = spread_ref[1, spread_rows, lanes]
                pairs = [
                    (jnp.where(lower_half, below, middle), jnp.where(lower_half, middle, above)),
                    (
                        jnp.where(y_low, gy, pltpu.roll(u, 8, 1)),
                        jnp.where(y_top, gy, pltpu.roll(u, 120, 1)),
                    ),
                    (
                        jnp.where(z_low, gz, pltpu.roll(u, 1, 1)),
                        jnp.where(z_top, gz, pltpu.roll(u, 127, 1)),
                    ),
                ]
                twice = u + u
                total = None
                for d in range(3):
                    lower, upper = pairs[d]
                    diffs[d].append(upper - lower)
                    term = speed_ref[d] * ((upper - twice) + lower)
                    total = term if total is None else total + term
                values.append(u)
                smooth.append(total)
            for i in range(variables):
                change = -smooth[i]
                for d in range(3):
                    for j in range(variables):
                        change = change + mix_ref[64 * d + 8 * i + j] * diffs[d][j]
                out_ref[i, rows, lanes] = values[i] - rate * change
        return carry

    lax.fori_loop(0, 8, rows_step, 0)
    if last:
        total = flow_ref[0] * out_ref[0]
        for v in range(1, variables):
            total = total + flow_ref[v] * out_ref[v]
        patches = sum_of_parts(product_of_parts(split_three(total), select_ref[...]))
        parts = jnp.concatenate(split_three(patches) + (segment_ref[...],), axis=1)
        sent = [product(place_ref[0], parts), product(place_ref[1], parts)]
        for k in range(2):
            extra_ref[:, 0, 128 * k : 128 * k + 128] = sum_of_parts(
                [sent[k][:, 128 * i : 128 * i + 128] for i in range(3)]
            )
        extra_ref[:, 0, 256:384] = jnp.where(
            iota((128, 128), 1) < 64, sent[0][:, 384:512], sent[1][:, 384:512]
        )
    else:
        write_faces(out_ref, select_ref, extra_ref)


SMEM_SPEC = pl.BlockSpec(memory_space=pltpu.SMEM)
VMEM_SPEC = pl.BlockSpec(memory_space=pltpu.VMEM)
INTERPRET = False


def on_chip(*values):
    if INTERPRET:
        return values
    return tuple(pltpu.with_memory_space_constraint(value, pltpu.VMEM) for value in values)


def make_faces(state_in, selection):
    return pl.pallas_call(
        faces_kernel,
        out_shape=jax.ShapeDtypeStruct(state_in.shape[:2] + (384,), jnp.float32),
        in_specs=[VMEM_SPEC] * 2,
        out_specs=VMEM_SPEC,
        interpret=INTERPRET,
    )(state_in, selection)


def advance(mix, speeds, flow, state_in, prev, own, following, pick, expand, rate, selection, place, segment, last):
    variables, blocks = state_in.shape[:2]
    (prev, following), shared = on_chip(prev, following), (pick, expand, rate, selection)
    if not last:
        own, *shared = on_chip(own, *shared)
    operands = (state_in, prev, own, following, *shared, place, segment)
    extra = (128, 1, 384) if last else (variables, blocks, 384)
    return pl.pallas_call(
        functools.partial(step_kernel, last=last),
        out_shape=(
            jax.ShapeDtypeStruct(state_in.shape, jnp.float32),
            jax.ShapeDtypeStruct(extra, jnp.float32),
        ),
        in_specs=[SMEM_SPEC] * 3 + [VMEM_SPEC] * 10,
        out_specs=(VMEM_SPEC, VMEM_SPEC),
        scratch_shapes=[
            pltpu.VMEM((2, 64 * variables, 256), jnp.bfloat16),
            pltpu.VMEM((2, 64 * variables, 512), jnp.float32),
            pltpu.VMEM((variables, 64, 128), jnp.float32),
        ],
        interpret=INTERPRET,
    )(
        mix,
        speeds,
        flow,
        *operands,
    )


def block_picks(neighbours, offset):
    blocks = neighbours.shape[0]
    local = jnp.where(
        neighbours >= 0, neighbours - offset, 3 * blocks + jnp.arange(blocks, dtype=jnp.int32)[:, None]
    )
    index = jnp.transpose(local).reshape(3, 2 * blocks)
    return (index[:, :, None] == iota((3, 2 * blocks, 4 * blocks), 2)).astype(jnp.bfloat16)


def wave_speeds(flux_derivative_matrices):
    return jnp.max(jnp.sum(jnp.abs(flux_derivative_matrices), axis=2), axis=1)


def transform_tables():
    column = np.arange(64)
    q, imaginary = 2 * (column // 8) + column % 2, column // 4 % 2 == 1
    s, r, n = np.arange(16), np.arange(64), np.arange(32)
    step = 2.0 * np.pi * np.outer(s, q) / 16
    twist = 2.0 * np.pi * np.outer(r, q) / NLON
    wave = 2.0 * np.pi * np.outer(n, r) / 64
    split = np.concatenate([np.cos(step), -np.sin(step)], axis=1)
    twiddle = np.stack([np.cos(twist), np.sin(twist)])
    forward = np.concatenate([np.cos(wave), np.sin(wave)], axis=1) / NLON
    backward = np.concatenate([np.cos(wave), np.sin(wave)], axis=0).T
    factor = np.where((n[:, None] == 0) & (q[None, :] == 0), 1.0, 2.0)
    untwist = np.stack(
        [
            np.where(imaginary, -np.sin(twist), np.cos(twist)),
            np.where(imaginary, -np.cos(twist), -np.sin(twist)),
        ]
    )
    of_latitude = [(column // 2 % 2 == latitude)[None, :] for latitude in range(2)]
    join = np.concatenate(
        [np.concatenate([np.cos(step) * own, np.sin(step) * own], axis=1) for own in of_latitude]
    )
    return [
        jnp.asarray(table.astype(np.float32))
        for table in (split, twiddle, forward, factor, backward, untwist, join)
    ]


def landing_of(codes, k):
    return codes[:, 64 * k : 64 * k + 16] == (iota((128, 16), 1) + 1).astype(jnp.float32)


def forward_kernel(got_ref, split_ref, twiddle_ref, forward_ref, grid_ref, send_ref):
    grid = None
    codes = got_ref[:, 256:384]
    for k in range(2):
        landing = landing_of(codes, k).astype(jnp.float32)
        part = exact(landing, got_ref[:, 128 * k : 128 * k + 128], 0, 0)
        grid = part if grid is None else grid + part
    grid_ref[...] = grid
    column = iota((64, 64), 1)
    split = split_ref[...]
    first, second = exact(grid[:, 0:64], split, 0, 0), exact(grid[:, 64:128], split, 0, 0)
    of_first = column // 2 % 2 == 0
    even = jnp.where(of_first, first[:, 0:64], second[:, 0:64])
    odd = jnp.where(of_first, first[:, 64:128], second[:, 64:128])
    turned_re = even * twiddle_ref[0] + odd * twiddle_ref[1]
    turned_im = odd * twiddle_ref[0] - even * twiddle_ref[1]
    real = column // 4 % 2 == 0
    both = jnp.concatenate(
        [jnp.where(real, turned_re, turned_im), jnp.where(real, turned_im, -turned_re)], axis=0
    )
    coef = exact(forward_ref[...], both)
    for part in range(8):
        send_ref[32 * part : 32 * part + 32, :] = coef[:, 8 * part : 8 * part + 8]


def backward_kernel(
    synth_ref, got_ref, factor_ref, backward_ref, untwist_ref, join_ref, grid_ref, back_ref, pair_ref
):
    for part in range(8):
        columns = slice(8 * part, 8 * part + 8)
        values = synth_ref[32 * part : 32 * part + 32, :]
        pair_ref[0:32, columns] = values
        pair_ref[32:64, columns] = jnp.concatenate([-values[:, 4:8], values[:, 0:4]], axis=1)
    factor = factor_ref[...]
    pair = pair_ref[...] * jnp.concatenate([factor, factor], axis=0)
    rows = exact(backward_ref[...], pair)
    turned = jnp.concatenate([rows * untwist_ref[0], rows * untwist_ref[1]], axis=1)
    joined = exact(join_ref[...], turned, 1, 1)
    grid_ref[:, 0:64] = joined[0:16]
    grid_ref[:, 64:128] = joined[16:32]
    parts = jnp.concatenate(split_three(grid_ref[...]), axis=1)
    codes = got_ref[:, 256:384]
    for k in range(2):
        found = product(landing_of(codes, k).astype(jnp.float32).astype(jnp.bfloat16), parts)
        back_ref[:, 0, 128 * k : 128 * k + 128] = sum_of_parts(
            [found[:, 128 * i : 128 * i + 128] for i in range(3)]
        )


def home_kernel(home_ref, place_ref, shell_ref):
    total = None
    for k in range(2):
        parts = jnp.concatenate(split_three(home_ref[:, 128 * k : 128 * k + 128]), axis=1)
        found = lax.dot_general(
            place_ref[k], parts, (((0,), (0,)), ((), ())), preferred_element_type=jnp.float32
        )
        part = sum_of_parts([found[:, 128 * i : 128 * i + 128] for i in range(3)])
        total = part if total is None else total + part
    shell_ref[...] = total


def run_kernel(kernel, operands, shapes, scratch=()):
    return pl.pallas_call(
        kernel,
        out_shape=tuple(jax.ShapeDtypeStruct(shape, jnp.float32) for shape in shapes),
        in_specs=[VMEM_SPEC] * len(operands),
        out_specs=tuple([VMEM_SPEC] * len(shapes)),
        scratch_shapes=[pltpu.VMEM(shape, jnp.float32) for shape in scratch],
        interpret=INTERPRET,
    )(*on_chip(*operands))


def legendre_start(sine_lat, orders):
    series_k = jnp.arange(1, DEGREES, dtype=jnp.int32).astype(jnp.float32)
    log_sums = jnp.concatenate(
        [
            jnp.zeros((1,), jnp.float32),
            jnp.cumsum(0.5 * jnp.log((2.0 * series_k + 1.0) / (2.0 * series_k))),
        ]
    )
    log_base = jnp.take(log_sums, orders)
    return jnp.exp(0.5 * math.log(0.5) + log_base + orders.astype(jnp.float32) * jnp.log(sine_lat))


def recurrence_factors(orders):
    degree = iota((DEGREES, orders.shape[0]), 0)
    order = jnp.broadcast_to(orders[None, :], degree.shape)
    degree_real, order_real = degree.astype(jnp.float32), order.astype(jnp.float32)
    ratio_up = jnp.sqrt(
        jnp.maximum(4.0 * degree_real * degree_real - 1.0, 1.0)
        / jnp.maximum(degree_real * degree_real - order_real * order_real, 1.0)
    )
    lower_deg = degree_real - 1.0
    ratio_back = jnp.sqrt(
        jnp.maximum(lower_deg * lower_deg - order_real * order_real, 0.0)
        / jnp.maximum(4.0 * lower_deg * lower_deg - 1.0, 1.0)
    )
    coef_prev = jnp.where(
        degree == order + 1,
        jnp.sqrt(2.0 * order_real + 3.0),
        jnp.where(degree >= order + 2, ratio_up, 0.0),
    )
    coef_before = jnp.where(degree >= order + 2, -ratio_up * ratio_back, 0.0)
    return coef_prev, coef_before


def spectral_kernel(
    first_ref, prev_ref, before_ref, gain_ref, re_ref, im_ref, diagonal_ref, cosine_ref, out_ref
):
    even = iota((8, 128), 0) % 2 == 0
    order = first_ref[0] + iota((8, 128), 0) % 2
    rows_re, rows_im = re_ref[...], im_ref[...]
    diagonal, cosine = diagonal_ref[...], cosine_ref[...]
    zero = jnp.zeros((8, 128), jnp.float32)

    def over_latitudes(value):
        value = value + pltpu.roll(value, 4, 0)
        value = value + pltpu.roll(value, 2, 0)
        return jnp.sum(value, axis=1, keepdims=True)

    def some_degrees(step, carried):
        previous, before, acc_re, acc_im = carried
        for inner in range(16):
            degree = 16 * step + inner
            up = jnp.where(even, prev_ref[2 * degree], prev_ref[2 * degree + 1])
            back = jnp.where(even, before_ref[2 * degree], before_ref[2 * degree + 1])
            present = (up * cosine) * previous + back * before
            present = jnp.where(order == degree, diagonal, present)
            gain = gain_ref[degree]
            acc_re = acc_re + (gain * over_latitudes(rows_re * present)) * present
            acc_im = acc_im + (gain * over_latitudes(rows_im * present)) * present
            previous, before = present, previous
        return previous, before, acc_re, acc_im

    carried = lax.fori_loop(0, DEGREES // 16, some_degrees, (zero, zero, zero, zero))
    acc_re, acc_im = carried[2], carried[3]
    top = iota((8, 128), 0) < 4
    out_ref[0] = jnp.where(top, acc_re, pltpu.roll(acc_im, 4, 0))
    out_ref[1] = jnp.where(top, pltpu.roll(acc_re, 4, 0), acc_im)


def solve_spectral(received, first_order, lat_total):
    rows = received.reshape(2, 128, 2, 4).transpose(2, 0, 3, 1).reshape(2, 8, 128)
    row, lane = iota((8, 128), 0), iota((8, 128), 1)
    lat_ids = 256 * (row // 4) + 2 * lane + row // 2 % 2
    colatitude = (lat_ids.astype(jnp.float32) + 0.5) * (math.pi / lat_total)
    cosine, sine = jnp.cos(colatitude), jnp.sin(colatitude)
    weights = math.pi / lat_total * sine
    orders = first_order + jnp.arange(2, dtype=jnp.int32)
    diagonal = legendre_start(sine, jnp.broadcast_to(jnp.tile(orders, 4)[:, None], (8, 128)))
    coef_prev, coef_before = recurrence_factors(orders)
    degree_real = jnp.arange(DEGREES, dtype=jnp.int32).astype(jnp.float32)
    gain = POT_GAIN / (degree_real * (degree_real + 1.0) + KAPPA2)
    both = pl.pallas_call(
        spectral_kernel,
        out_shape=jax.ShapeDtypeStruct((2, 8, 128), jnp.float32),
        in_specs=[SMEM_SPEC] * 4 + [VMEM_SPEC] * 4,
        out_specs=VMEM_SPEC,
        interpret=INTERPRET,
    )(
        orders[0:1],
        coef_prev.reshape(-1),
        coef_before.reshape(-1),
        gain,
        *on_chip(rows[0] * weights, rows[1] * weights, diagonal, cosine),
    )
    return both.transpose(0, 2, 1).reshape(256, 8)


def body(
    invariant_fluid_quantities,
    flux_derivative_matrices,
    levels,
    neighbours,
    block_latitude_band,
    block_longitude_segment,
    parallel_flow_coefficients,
):
    grp_size = lax.axis_size("grp")
    core_size = lax.axis_size("cores")
    device_total = grp_size * core_size
    block_portion = invariant_fluid_quantities.shape[1]
    state_variables = invariant_fluid_quantities.shape[0]
    device = lax.axis_index(("grp", "cores"))
    speeds = wave_speeds(flux_derivative_matrices)
    rate_block = COURANT * jnp.exp2(levels.astype(jnp.float32) - (LEVELS - 1)) / jnp.max(speeds)
    offset = (device - 1) * block_portion
    picks = block_picks(neighbours, offset)
    selection, expand = face_selection(), ghost_expansion()
    rate = jnp.broadcast_to(rate_block[:, None], (block_portion, 128))
    mix = 0.5 * flux_derivative_matrices.reshape(-1)
    half_speeds = 0.5 * speeds
    band_index = block_latitude_band[:, 0]
    block_ids = jnp.arange(block_portion, dtype=jnp.int32)
    earlier = (band_index[None, :] == band_index[:, None]) & (
        block_ids[None, :] < block_ids[:, None]
    )
    rank_in_band = jnp.sum(earlier.astype(jnp.int32), axis=1)
    shape = (2, grp_size, block_portion)
    place = (
        (band_index[None, None, :] == iota(shape, 1)) & (rank_in_band[None, None, :] == iota(shape, 0))
    ).astype(jnp.bfloat16)
    segment = jnp.broadcast_to(
        (block_longitude_segment + 1).astype(jnp.bfloat16)[:, None], (block_portion, 128)
    )
    parallel_flow_charge = invariant_fluid_quantities
    faces = make_faces(parallel_flow_charge, selection)
    for section_index in range(STEPS):
        last = section_index == STEPS - 1
        parallel_flow_charge, faces = advance(
            mix,
            half_speeds,
            parallel_flow_coefficients,
            parallel_flow_charge,
            passed_along(faces, ("grp", "cores"), 1),
            faces,
            passed_along(faces, ("grp", "cores"), -1),
            picks,
            expand,
            rate,
            patch_selection() if last else selection,
            place,
            segment,
            last,
        )
    split, twiddle, forward, factor, backward, untwist, join = transform_tables()
    got = lax.all_to_all(faces, "grp", split_axis=0, concat_axis=0, tiled=True)
    got = got.reshape(grp_size, 384)
    fac_segments, coef = run_kernel(
        forward_kernel, (got, split, twiddle, forward), ((16, 128), (device_total, 8))
    )
    axes = ("grp", "cores")
    received = lax.all_to_all(coef, axes, split_axis=0, concat_axis=0, tiled=True)
    synth = solve_spectral(received, 16 * (device % 32) + 2 * (device // 32), LAT_DEV * device_total)
    returned = lax.all_to_all(synth, axes, split_axis=0, concat_axis=0, tiled=True)
    grid_segments, back = run_kernel(
        backward_kernel,
        (returned, got, factor, backward, untwist, join),
        ((16, 128), (grp_size, 1, 256)),
        scratch=((64, 64),),
    )
    home = lax.all_to_all(back, "grp", split_axis=0, concat_axis=0, tiled=True)
    home = home.reshape(grp_size, 256)
    (shell_potential,) = run_kernel(home_kernel, (home, place), ((block_portion, 128),))
    fac_local, potential_local = (
        jnp.swapaxes(grid.reshape(16, LAT_DEV, 64), 0, 1).reshape(LAT_DEV, NLON)
        for grid in (fac_segments, grid_segments)
    )
    return (parallel_flow_charge, fac_local, potential_local, shell_potential)


def solution(mesh):
    placed = (
        P(None, ("grp", "cores"), None),
        P(),
        P(("grp", "cores")),
        P(("grp", "cores"), None),
        P(("grp", "cores"), None),
        P(("grp", "cores")),
        P(),
    )
    return jax.shard_map(
        body,
        mesh=mesh,
        in_specs=placed,
        out_specs=(
            P(None, ("grp", "cores"), None),
            P(("grp", "cores"), None),
            P(("grp", "cores"), None),
            P(("grp", "cores"), None),
        ),
        check_vma=False,
    )
```
